512 devices in a mesh: rep: 4 (over x), exp: 128 (over z, y, core).
Axes of the slice: x: 4, y: 8, z: 8, core: 2. Of those that a mesh axis runs over, the one named last changes fastest.
Arguments:
- tokens: bfloat16 [16384, 2048], P('exp', 'rep'), may hold values from -6 to 6
- expert_ids: int32 [16384, 8], P('exp'), may hold values from 0 to 127, all different within a row; in each aligned block of 128 rows (0 to 127, 128 to 255, ...) at most 12 rows name the same one
- route_weights: float32 [16384, 8], P('exp'), may hold values from 0.05 to 1
- w_gate: bfloat16 [128, 768, 2048], P('exp', None, 'rep'), may hold values from -0.125 to 0.125
- w_up: bfloat16 [128, 768, 2048], P('exp', None, 'rep'), may hold values from -0.125 to 0.125
- w_down: bfloat16 [128, 768, 2048], P('exp', None, 'rep'), may hold values from -0.21875 to 0.21875
Outputs:
- mixed: bfloat16 [16384, 2048], P('exp', 'rep')
The draws below stay inside these ranges and needn't reach their ends.
Inputs may be any that keep to these rules, and one draw needn't show every extreme that they name: `expert_ids`: each token names 8 different experts. Within the rows of one index of exp (aligned blocks of 128 tokens) no expert is named more than 12 times, a bound that some block reaches.
All inputs are finite; a program needn't handle non-finite values.
Results may differ from the reference program's by a relative error of at most 0.0058.
Values may be sent and summed in bfloat16 or wider, within the bound.
A program may use at most 64 MiB of HBM per device.

```python
import math
import jax
import jax.numpy as jnp
import numpy as np
from jax import lax

D = 2048
FF = 768
EXPERTS = 128
TOP = 8
TOK_DEV = 128
CAP = 12
TOKENS = 16384


def block_scale(own_key, extent, shards, least, largest):
    factor_of, own = 1.0, jax.random.fold_in(own_key, 6)
    for axis_at, blocks in shards:
        draws = jnp.exp(jax.random.uniform(jax.random.fold_in(own, axis_at), (blocks,), jnp.float32, least / len(shards), largest / len(shards)))
        factor_of = factor_of * jnp.repeat(draws, extent[axis_at] // blocks).reshape([-1 if axis == axis_at else 1 for axis in range(len(extent))])
    return factor_of


def routed_block(rng, own, number, rows, count, top, most, slope):
    sequence = jax.random.permutation(rng, count)
    packed, common = shares(count, rows * top, most, slope, True), shares(count, rows * top, most, slope, False)
    places = jnp.arange(count)

    def named(lengths, offset_by):
        used = int((lengths > 0).sum())
        fixed = max(1, used // 4)
        shifted = fixed + (places - fixed + offset_by * (used - fixed)) % max(1, count - fixed)
        return jnp.zeros((count,), jnp.int32).at[sequence[jnp.where(places < fixed, places, shifted)]].set(jnp.asarray(lengths, jnp.int32))

    lengths = jnp.where(number % 4 == 0, named(packed, number // 4), named(common, number - number // 4 - 1))
    mixed = jax.random.permutation(jax.random.fold_in(own, 3), count)
    donor, taker = mixed[0:count // 2 * 2:2], mixed[1:count // 2 * 2:2]
    slack = jnp.minimum(lengths[donor] - 1, most - lengths[taker]) // 2
    slack = jnp.where((donor == sequence[0]) | (taker == sequence[0]) | (lengths[taker] == 0), 0, jnp.maximum(slack, 0))
    shifted = jax.random.randint(jax.random.fold_in(own, 4), (count // 2,), 0, 1 << 20) % (slack + 1)
    lengths = lengths.at[donor].add(-shifted).at[taker].add(shifted)
    members = jnp.searchsorted(jnp.cumsum(lengths), jnp.arange(rows * top), side="right").astype(jnp.int32)
    table = members.reshape(top, rows).T
    table = table[jax.random.permutation(jax.random.fold_in(own, 1), rows)]
    offset_by = jax.random.randint(jax.random.fold_in(own, 2), (rows, 1), 0, top)
    return jnp.take_along_axis(table, (jnp.arange(top)[None, :] + offset_by) % top, axis=1)


def shares(number_of, total, bound, lean, full):
    weights = [(1 << 20) // math.isqrt(grade ** lean) + 1 for grade in range(1, number_of + 1)]
    largest = bound if full else min(bound, max(-(-total // number_of), total * weights[0] // sum(weights)))
    least = 1 if total - largest >= number_of - 1 else 0
    given, rest = [largest] + [least] * (number_of - 1), total - largest - least * (number_of - 1)
    while rest > 0:
        movable = [i for i in range(1, number_of) if given[i] < largest] or [i for i in range(1, number_of) if given[i] < bound]
        mass, budget = sum([weights[i] for i in movable]), rest
        for i in movable:
            addition = min(bound - given[i], max(1, budget * weights[i] // mass), rest)
            given[i] = given[i] + addition
            rest = rest - addition
    return np.array(given)


def gaussian(key, extent, scale, most, shards=(), kind=jnp.bfloat16):
    entries = scale * jax.random.normal(key, extent, jnp.float32)
    if shards:
        entries = entries * block_scale(key, extent, shards, -0.22, 0.18)
    return jnp.clip(entries, -most, most).astype(kind)


def setup_inputs(seed: int = 0) -> dict:
    seeds = jax.random.split(jax.random.key(seed), 7)
    tokens = gaussian(seeds[0], (TOKENS, D), 1.0, 6.0, ((0, 128), (1, 4)))
    expert_ids_keys = jax.random.split(jax.random.fold_in(seeds[1], 1), TOKENS // TOK_DEV)
    expert_ids_turns = jax.random.permutation(jax.random.fold_in(seeds[1], 3), TOKENS // TOK_DEV)
    expert_ids = jax.vmap(lambda own, number: routed_block(jax.random.fold_in(seeds[1], 2), own, number, TOK_DEV, EXPERTS, TOP, CAP, 2))(expert_ids_keys, expert_ids_turns).reshape((TOKENS, TOP))
    route_weights = jnp.clip(jnp.exp(math.log(1.0) - 2.9957323 * jax.random.uniform(seeds[2], (TOKENS, TOP), jnp.float32) ** block_scale(seeds[2], (TOKENS, TOP), ((0, 128),), -0.2, 0.2)), 0.05, 1.0)
    w_gate = gaussian(seeds[3], (EXPERTS, FF, D), D ** -0.5, 0.125, ((0, 128), (2, 4)))
    w_up = gaussian(seeds[4], (EXPERTS, FF, D), D ** -0.5, 0.125, ((0, 128), (2, 4)))
    w_down = gaussian(seeds[5], (EXPERTS, FF, D), FF ** -0.5, 0.21875, ((0, 128), (2, 4)))
    return {"tokens": tokens, "expert_ids": expert_ids, "route_weights": route_weights, "w_gate": w_gate, "w_up": w_up, "w_down": w_down}


def block_slots(block_ids):
    onehot = (block_ids[:, None] == jnp.arange(EXPERTS, dtype=jnp.int32)[None, :]).astype(jnp.int32)
    before = jnp.cumsum(onehot, axis=0) - onehot
    return jnp.sum(before * onehot, axis=1).astype(jnp.int32)


def reference(tokens, expert_ids, route_weights, w_gate, w_up, w_down):
    tok_total = expert_ids.shape[0]
    top_count = expert_ids.shape[1]
    blocks = tok_total // TOK_DEV
    per_block = expert_ids.reshape(blocks, TOK_DEV * top_count)
    slot_ids = lax.map(block_slots, per_block).reshape(-1)
    assigned = expert_ids.reshape(-1)
    block_index = (jnp.arange(tok_total * top_count) // (TOK_DEV * top_count)).astype(jnp.int32)
    position = (block_index * CAP + slot_ids).astype(jnp.int32)
    token_source = (jnp.arange(tok_total * top_count) // top_count).astype(jnp.int32)
    probs = route_weights / jnp.sum(route_weights, axis=1, keepdims=True)
    norm_weight = probs.reshape(-1)
    rows_expert = blocks * CAP
    token_table = jnp.zeros((EXPERTS, rows_expert), jnp.int32).at[assigned, position].set(token_source)
    weight_table = jnp.zeros((EXPERTS, rows_expert), jnp.float32).at[assigned, position].set(norm_weight)

    def add_expert(accumulated, expert_index):
        row_tokens = token_table[expert_index]
        row_scale = weight_table[expert_index]
        chosen = tokens[row_tokens]
        gate_part = jnp.dot(chosen, w_gate[expert_index].T, preferred_element_type=jnp.float32)
        up_part = jnp.dot(chosen, w_up[expert_index].T, preferred_element_type=jnp.float32)
        hidden = (jax.nn.silu(gate_part) * up_part).astype(jnp.bfloat16)
        expert_out = jnp.dot(hidden, w_down[expert_index], preferred_element_type=jnp.float32).astype(jnp.bfloat16)
        expert_out = lax.optimization_barrier(expert_out).astype(jnp.float32)
        return accumulated.at[row_tokens].add(expert_out * row_scale[:, None]), None

    start_sum = jnp.zeros((tok_total, tokens.shape[1]), jnp.float32)
    accumulated, _ = lax.scan(add_expert, start_sum, jnp.arange(EXPERTS, dtype=jnp.int32))
    return accumulated.astype(jnp.bfloat16)
```

```python
import functools

import jax
import jax.numpy as jnp
from jax import lax
from jax.experimental import pallas as pl
from jax.experimental.pallas import tpu as pltpu
from jax.sharding import PartitionSpec as P

MESH = pl.DeviceIdType.MESH
BF16 = jnp.bfloat16
F32 = jnp.float32
CAP = 12
QUADS = 3
SPAN = 16
LANES = 128
BLOCKS = 4
CORES = 2
STAGES = 5


def signed_step(place, size):
    return (size + (1 - 2 * ((place + 1) % 2)) * ((place + 1) // 2)) % size


def place_of(offset, size):
    return jnp.where(
        offset == 0, 0, jnp.where(2 * offset <= size, 2 * offset - 1, 2 * (size - offset))
    )


def dot(a, b):
    return jnp.dot(a, b, preferred_element_type=F32)


def dot_t(a, b):
    return lax.dot_general(a, b, (((1,), (1,)), ((), ())), preferred_element_type=F32)


def kernel(
    sizes,
    tok,
    ids,
    route,
    wg_any,
    wu_any,
    wd_any,
    out,
    wg,
    wu,
    wd,
    perm,
    perm_t,
    slot_t,
    slot_tok,
    prob_tok,
    send,
    recv,
    back,
    home,
    table,
    part,
    part16,
    far_in,
    near_in,
    relay,
    relay_in,
    hid,
    w_sem,
    send_sem,
    recv_sem,
    back_sem,
    home_sem,
    x_send,
    x_recv,
):
    n_z, n_y, n_rep = sizes
    experts = n_z * SPAN
    ff = wg.shape[0]
    half = ff // 2
    quarter = SPAN * CAP // n_rep
    me, rep = lax.axis_index("exp"), lax.axis_index("rep")
    my_z, my_y, my_c = me // SPAN, (me // CORES) % n_y, me % CORES
    right, left, opp = (rep + 1) % n_rep, (rep + n_rep - 1) % n_rep, (rep + 2) % n_rep

    def peer(k, sign):
        place_z, place_y, flip = k // SPAN, (k % SPAN) // CORES, k % CORES
        z = (my_z + n_z + sign * signed_step(place_z, n_z)) % n_z
        y = (my_y + n_y + sign * signed_step(place_y, n_y)) % n_y
        return (z * n_y + y) * CORES + (my_c + flip) % CORES

    barrier = pltpu.get_barrier_semaphore()

    @pl.loop(1, experts)
    def _(k):
        pl.semaphore_signal(barrier, inc=1, device_id={"exp": peer(k, 1)}, device_id_type=MESH)

    for side in (left, right):
        pl.semaphore_signal(barrier, inc=1, device_id={"rep": side}, device_id_type=MESH)

    weights = [
        pltpu.make_async_copy(src.at[0], dst, w_sem.at[i])
        for i, (src, dst) in enumerate(((wg_any, wg), (wu_any, wu), (wd_any, wd)))
    ]
    for copy in weights:
        copy.start()

    row = lax.broadcasted_iota(jnp.int32, (256, 256), 0)
    col = lax.broadcasted_iota(jnp.int32, (256, 256), 1)
    perm[...] = (
        col == (row & 3) * 64 + ((row >> 2) & 3) * 16 + (row >> 4)
    ).astype(F32).astype(BF16)
    perm_t[...] = (
        row == (col & 3) * 64 + ((col >> 2) & 3) * 16 + (col >> 4)
    ).astype(F32).astype(BF16)

    chosen = ids[...]
    rows = chosen.shape[0]
    off_z = ((chosen >> 4) - my_z + n_z) & (n_z - 1)
    off_y = (((chosen >> 1) & (n_y - 1)) - my_y + n_y) & (n_y - 1)
    off_c = ((chosen & 1) - my_c + CORES) & 1
    number = place_of(off_z, n_z) * SPAN + place_of(off_y, n_y) * CORES + off_c
    probs = route[...] / jnp.sum(route[...], axis=1, keepdims=True)
    lane = lax.broadcasted_iota(jnp.int32, (rows, experts), 1)
    named = jnp.zeros((rows, experts), F32)
    prob = jnp.zeros((rows, experts), F32)
    for j in range(chosen.shape[1]):
        hit = number[:, j : j + 1] == lane
        named = named + jnp.where(hit, 1.0, 0.0)
        prob = prob + jnp.where(hit, probs[:, j : j + 1], 0.0)
    t_row = lax.broadcasted_iota(jnp.int32, (rows, rows), 0)
    t_col = lax.broadcasted_iota(jnp.int32, (rows, rows), 1)
    below = (t_col < t_row).astype(F32).astype(BF16)
    slot = dot(below, named.astype(BF16))
    slot = jnp.where(named > 0.5, slot, -1.0)
    slot_tok[...] = slot
    prob_tok[...] = prob
    slot_t[...] = slot.T

    pl.semaphore_wait(barrier, experts + 1)

    def pack(rows2d, place, g):
        stacked = jnp.concatenate(
            [
                jnp.concatenate(
                    [rows2d[64 * q : 64 * q + 64, LANES * b : LANES * (b + 1)] for b in range(BLOCKS)],
                    axis=0,
                )
                for q in range(QUADS)
            ],
            axis=1,
        )
        tiles = dot(perm[...], stacked).astype(BF16)
        for q in range(QUADS):
            place[pl.ds(g * SPAN, SPAN), q] = tiles[:, LANES * q : LANES * (q + 1)].reshape(
                SPAN, SPAN, LANES
            )

    def unpack(place, g):
        tiles = jnp.concatenate(
            [place[pl.ds(g * SPAN, SPAN), q].reshape(256, LANES) for q in range(QUADS)], axis=1
        )
        return dot(perm_t[...], tiles).astype(BF16)

    @pl.loop(0, n_z)
    def _(g):
        slots = slot_t[pl.ds(g * SPAN, SPAN), :]
        onehot = jnp.concatenate(
            [(slots == float(s)).astype(F32).astype(BF16) for s in range(CAP)], axis=0
        )
        pack(dot(onehot, tok[...]).astype(BF16), send, g)

        @pl.loop(0, SPAN)
        def _(h):
            k = g * SPAN + h

            @pl.when(k > 0)
            def _():
                pltpu.make_async_remote_copy(
                    src_ref=send.at[k],
                    dst_ref=recv.at[k],
                    send_sem=send_sem,
                    recv_sem=recv_sem.at[g],
                    device_id={"exp": peer(k, 1)},
                    device_id_type=MESH,
                ).start()

            @pl.when(k == 0)
            def _():
                pltpu.make_async_copy(send.at[0], recv.at[0], recv_sem.at[0]).start()

    for copy in weights:
        copy.wait()

    def across(kind, c, src, dst, side):
        return pltpu.make_async_remote_copy(
            src_ref=src,
            dst_ref=dst,
            send_sem=x_send.at[kind, c],
            recv_sem=x_recv.at[kind, c],
            device_id={"rep": side},
            device_id_type=MESH,
        )

    def far(c):
        return (
            across(0, c, part16.at[0, c, opp], far_in.at[0, c], right),
            across(1, c, part16.at[1, c, opp], far_in.at[1, c], left),
        )

    def near(c):
        return (
            across(2, c, part16.at[1, c, right], near_in.at[1, c], right),
            across(3, c, part16.at[0, c, left], near_in.at[0, c], left),
        )

    def relayed(c):
        return (
            across(4, c, relay.at[0, c], relay_in.at[0, c], right),
            across(5, c, relay.at[1, c], relay_in.at[1, c], left),
        )

    def hidden_out(c):
        return (
            across(6, c, hid.at[c, rep], hid.at[c, rep], right),
            across(7, c, hid.at[c, rep], hid.at[c, rep], left),
        )

    def hidden_in(c):
        return (
            across(6, c, hid.at[c, left], hid.at[c, left], right),
            across(7, c, hid.at[c, right], hid.at[c, right], left),
        )

    def onward(c):
        return (
            across(8, c, hid.at[c, left, :, pl.ds(0, half)], hid.at[c, left, :, pl.ds(0, half)], right),
            across(9, c, hid.at[c, right, :, pl.ds(half, half)], hid.at[c, right, :, pl.ds(half, half)], left),
        )

    def onward_in(c):
        return (
            across(8, c, hid.at[c, opp, :, pl.ds(0, half)], hid.at[c, opp, :, pl.ds(0, half)], right),
            across(9, c, hid.at[c, opp, :, pl.ds(half, half)], hid.at[c, opp, :, pl.ds(half, half)], left),
        )

    def start(copies):
        for copy in copies:
            copy.start()

    def arrive(copies):
        for copy in copies:
            copy.wait_recv()

    def multiply(c):
        group = recv.at[pl.ds(c * SPAN, SPAN)]
        pltpu.make_async_copy(group, group, recv_sem.at[c]).wait()
        tiles = unpack(recv, c)
        x = jnp.concatenate(
            [
                jnp.concatenate(
                    [tiles[64 * b : 64 * b + 64, LANES * q : LANES * (q + 1)] for b in range(BLOCKS)],
                    axis=1,
                )
                for q in range(QUADS)
            ],
            axis=0,
        )
        for side, w in enumerate((wg, wu)):
            product = dot_t(x, w[...])
            for owner in range(n_rep):
                share = product[quarter * owner : quarter * (owner + 1)]
                part[side, c, owner] = share
                part16[side, c, owner] = share.astype(BF16)
        start(far(c))
        start(near(c))

    def add_on(c):
        arrive(far(c))
        relay[0, c] = (part[0, c, right] + far_in[0, c].astype(F32)).astype(BF16)
        relay[1, c] = (part[1, c, left] + far_in[1, c].astype(F32)).astype(BF16)
        start(relayed(c))

    def activate(c):
        arrive(near(c))
        arrive(relayed(c))
        gate = part[0, c, rep] + near_in[0, c].astype(F32) + relay_in[0, c].astype(F32)
        up = part[1, c, rep] + near_in[1, c].astype(F32) + relay_in[1, c].astype(F32)
        hid[c, rep] = (gate / (1.0 + jnp.exp(-gate)) * up).astype(BF16)
        start(hidden_out(c))

    def forward(c):
        arrive(hidden_in(c))
        start(onward(c))

    def down(c):
        arrive(onward_in(c))
        rows2d = dot(hid[c].reshape(n_rep * quarter, ff), wd[...]).astype(BF16)
        pack(rows2d, back, c)

        @pl.loop(0, SPAN)
        def _(h):
            k = c * SPAN + h

            @pl.when(k > 0)
            def _():
                pltpu.make_async_remote_copy(
                    src_ref=back.at[k],
                    dst_ref=home.at[k],
                    send_sem=back_sem,
                    recv_sem=home_sem.at[c],
                    device_id={"exp": peer(k, -1)},
                    device_id_type=MESH,
                ).start()

            @pl.when(k == 0)
            def _():
                pltpu.make_async_copy(back.at[0], home.at[0], home_sem.at[0]).start()

    @pl.loop(0, n_z + STAGES - 1)
    def _(i):
        for age, stage in ((4, down), (3, forward), (2, activate), (1, add_on), (0, multiply)):

            @pl.when((i >= age) & (i < n_z + age))
            def _(age=age, stage=stage):
                stage(i - age)

    @pl.loop(0, n_z)
    def _(c):
        group = home.at[pl.ds(c * SPAN, SPAN)]
        pltpu.make_async_copy(group, group, home_sem.at[c]).wait()
        tiles = unpack(home, c)
        for q in range(QUADS):
            for s in range(4):
                for b in range(BLOCKS):
                    table[
                        pl.ds((4 * q + s) * experts + c * SPAN, SPAN), LANES * b : LANES * (b + 1)
                    ] = tiles[64 * b + 16 * s : 64 * b + 16 * s + 16, LANES * q : LANES * (q + 1)]

    slot, prob = slot_tok[...], prob_tok[...]
    mix = jnp.concatenate(
        [jnp.where(slot == float(s), prob, 0.0) for s in range(CAP)], axis=1
    )
    high = mix.astype(BF16)
    low = (mix - high.astype(F32)).astype(BF16)
    out[...] = (dot(high, table[...]) + dot(low, table[...])).astype(BF16)

    sent = send.at[pl.ds(1, experts - 1)]
    pltpu.make_async_copy(sent, sent, send_sem).wait()
    returned = back.at[pl.ds(1, experts - 1)]
    pltpu.make_async_copy(returned, returned, back_sem).wait()

    @pl.loop(0, n_z)
    def _(c):
        for copies in (far(c), near(c), relayed(c), hidden_out(c), onward(c)):
            for copy in copies:
                copy.wait_send()


def local(sizes, tokens, expert_ids, route_weights, w_gate, w_up, w_down):
    n_z, n_y, n_rep = sizes
    experts = n_z * SPAN
    rows, width = tokens.shape
    ff = w_gate.shape[1]
    quarter = SPAN * CAP // n_rep
    messages = pltpu.VMEM((experts, QUADS, SPAN, LANES), BF16)
    pair = pltpu.VMEM((2, n_z, quarter, ff), BF16)
    vmem = pl.BlockSpec(memory_space=pltpu.VMEM)
    anywhere = pl.BlockSpec(memory_space=pl.ANY)
    return pl.pallas_call(
        functools.partial(kernel, sizes),
        out_shape=jax.ShapeDtypeStruct((rows, width), BF16),
        in_specs=[vmem] * 3 + [anywhere] * 3,
        out_specs=vmem,
        scratch_shapes=[
            pltpu.VMEM((ff, width), BF16),
            pltpu.VMEM((ff, width), BF16),
            pltpu.VMEM((ff, width), BF16),
            pltpu.VMEM((256, 256), BF16),
            pltpu.VMEM((256, 256), BF16),
            pltpu.VMEM((experts, rows), F32),
            pltpu.VMEM((rows, experts), F32),
            pltpu.VMEM((rows, experts), F32),
            messages,
            messages,
            messages,
            messages,
            pltpu.VMEM((CAP * experts, width), BF16),
            pltpu.VMEM((2, n_z, n_rep, quarter, ff), F32),
            pltpu.VMEM((2, n_z, n_rep, quarter, ff), BF16),
            pair,
            pair,
            pair,
            pair,
            pltpu.VMEM((n_z, n_rep, quarter, ff), BF16),
            pltpu.SemaphoreType.DMA((3,)),
            pltpu.SemaphoreType.DMA,
            pltpu.SemaphoreType.DMA((n_z,)),
            pltpu.SemaphoreType.DMA,
            pltpu.SemaphoreType.DMA((n_z,)),
            pltpu.SemaphoreType.DMA((10, n_z)),
            pltpu.SemaphoreType.DMA((10, n_z)),
        ],
        compiler_params=pltpu.CompilerParams(
            collective_id=0, has_side_effects=True, vmem_limit_bytes=58 * 1024 * 1024
        ),
    )(tokens, expert_ids, route_weights, w_gate, w_up, w_down)


def solution(mesh):
    n_rep, experts = mesh.shape["rep"], mesh.shape["exp"]
    sizes = (experts // SPAN, SPAN // CORES, n_rep)
    return jax.shard_map(
        functools.partial(local, sizes),
        mesh=mesh,
        in_specs=(
            P("exp", "rep"),
            P("exp", None),
            P("exp", None),
            P("exp", None, "rep"),
            P("exp", None, "rep"),
            P("exp", None, "rep"),
        ),
        out_specs=P("exp", "rep"),
        check_vma=False,
    )
```

```python
import functools

import jax
import jax.numpy as jnp
from jax import lax
from jax.experimental import pallas as pl
from jax.experimental.pallas import tpu as pltpu
from jax.sharding import PartitionSpec as P

MESH = pl.DeviceIdType.MESH
BF16 = jnp.bfloat16
F32 = jnp.float32
CAP = 12
QUADS = 3
SPAN = 16
LANES = 128
BLOCKS = 4
CORES = 2
STAGES = 5


def signed_step(place):
    after = place + 1
    if isinstance(place, int):
        return (1 - 2 * (after % 2)) * (after // 2)
    return (1 - 2 * lax.rem(after, 2)) * lax.div(after, 2)


def place_of(offset, size):
    return jnp.where(
        offset == 0, 0, jnp.where(2 * offset <= size, 2 * offset - 1, 2 * (size - offset))
    )


def dot(a, b):
    return jnp.dot(a, b, preferred_element_type=F32)


def dot_t(a, b):
    return lax.dot_general(a, b, (((1,), (1,)), ((), ())), preferred_element_type=F32)


def kernel(
    sizes,
    tok,
    ids,
    route,
    wg_any,
    wu_any,
    wd_any,
    out,
    wg,
    wu,
    wd,
    perm,
    perm_t,
    slot_t,
    prob_t,
    send,
    recv,
    back,
    home,
    table,
    part,
    part16,
    far_in,
    near_in,
    relay,
    relay_in,
    hid,
    w_sem,
    send_sem,
    recv_sem,
    back_sem,
    home_sem,
    x_send,
    x_recv,
):
    n_z, n_y, n_rep = sizes
    experts = n_z * SPAN
    ff = wg.shape[0]
    half = ff // 2
    quarter = SPAN * CAP // n_rep
    me, rep = lax.axis_index("exp"), lax.axis_index("rep")
    my_z, my_y, my_c = lax.div(me, SPAN), lax.rem(lax.div(me, CORES), n_y), lax.rem(me, CORES)
    right, left, opp = (lax.rem(rep + step, n_rep) for step in (1, n_rep - 1, 2))

    def spots(sign):
        return [
            lax.rem(my_y + n_y + sign * signed_step(h // CORES), n_y) * CORES
            + lax.rem(my_c + h % CORES, CORES)
            for h in range(SPAN)
        ]

    def plane(g, sign):
        return lax.rem(my_z + n_z + sign * signed_step(g), n_z) * SPAN

    ahead, behind = spots(1), spots(-1)

    barrier = pltpu.get_barrier_semaphore()

    @pl.loop(0, n_z)
    def _(g):
        base = plane(g, 1)
        for h in range(SPAN):

            def greet(h=h):
                pl.semaphore_signal(
                    barrier, inc=1, device_id={"exp": base + ahead[h]}, device_id_type=MESH
                )

            if h:
                greet()
            else:
                pl.when(g > 0)(greet)

    for side in (left, right):
        pl.semaphore_signal(barrier, inc=1, device_id={"rep": side}, device_id_type=MESH)

    weights = [
        pltpu.make_async_copy(src.at[0], dst, w_sem.at[i])
        for i, (src, dst) in enumerate(((wg_any, wg), (wu_any, wu), (wd_any, wd)))
    ]
    for copy in weights:
        copy.start()

    row = lax.broadcasted_iota(jnp.int32, (256, 256), 0)
    col = lax.broadcasted_iota(jnp.int32, (256, 256), 1)
    perm[...] = (
        col == (row & 3) * 64 + ((row >> 2) & 3) * 16 + (row >> 4)
    ).astype(F32).astype(BF16)
    perm_t[...] = (
        row == (col & 3) * 64 + ((col >> 2) & 3) * 16 + (col >> 4)
    ).astype(F32).astype(BF16)

    chosen = ids[...]
    rows = chosen.shape[1]
    off_z = ((chosen >> 4) - my_z + n_z) & (n_z - 1)
    off_y = (((chosen >> 1) & (n_y - 1)) - my_y + n_y) & (n_y - 1)
    off_c = ((chosen & 1) - my_c + CORES) & 1
    number = place_of(off_z, n_z) * SPAN + place_of(off_y, n_y) * CORES + off_c
    probs = route[...] / jnp.sum(route[...], axis=0, keepdims=True)
    place = lax.broadcasted_iota(jnp.int32, (experts, rows), 0)
    named = jnp.zeros((experts, rows), F32)
    prob = jnp.zeros((experts, rows), F32)
    for j in range(chosen.shape[0]):
        hit = number[j : j + 1, :] == place
        named = named + jnp.where(hit, 1.0, 0.0)
        prob = prob + jnp.where(hit, probs[j : j + 1, :], 0.0)
    t_row = lax.broadcasted_iota(jnp.int32, (rows, rows), 0)
    t_col = lax.broadcasted_iota(jnp.int32, (rows, rows), 1)
    earlier = (t_row < t_col).astype(F32).astype(BF16)
    slot_t[...] = jnp.where(named > 0.5, dot(named.astype(BF16), earlier), -1.0)
    prob_t[...] = prob

    pl.semaphore_wait(barrier, experts + 1)

    def deliver(g, sign, spot, src, dst, out_sem, in_sem):
        base = plane(g, sign)
        for h in range(SPAN):

            def go(h=h):
                pltpu.make_async_remote_copy(
                    src_ref=src.at[g * SPAN + h],
                    dst_ref=dst.at[g * SPAN + h],
                    send_sem=out_sem,
                    recv_sem=in_sem.at[g],
                    device_id={"exp": base + spot[h]},
                    device_id_type=MESH,
                ).start()

            if h:
                go()
            else:
                pl.when(g > 0)(go)

                @pl.when(g == 0)
                def _():
                    pltpu.make_async_copy(src.at[0], dst.at[0], in_sem.at[0]).start()

    def pack(rows2d, place, g):
        stacked = jnp.concatenate(
            [
                jnp.concatenate(
                    [rows2d[64 * q : 64 * q + 64, LANES * b : LANES * (b + 1)] for b in range(BLOCKS)],
                    axis=0,
                )
                for q in range(QUADS)
            ],
            axis=1,
        )
        tiles = dot(perm[...], stacked).astype(BF16)
        for q in range(QUADS):
            place[pl.ds(g * SPAN, SPAN), q] = tiles[:, LANES * q : LANES * (q + 1)].reshape(
                SPAN, SPAN, LANES
            )

    def unpack(place, g):
        tiles = jnp.concatenate(
            [place[pl.ds(g * SPAN, SPAN), q].reshape(256, LANES) for q in range(QUADS)], axis=1
        )
        return dot(perm_t[...], tiles).astype(BF16)

    @pl.loop(0, n_z)
    def _(g):
        slots = slot_t[pl.ds(g * SPAN, SPAN), :]
        onehot = jnp.concatenate(
            [(slots == float(s)).astype(F32).astype(BF16) for s in range(CAP)], axis=0
        )
        pack(dot(onehot, tok[...]).astype(BF16), send, g)

        deliver(g, 1, ahead, send, recv, send_sem, recv_sem)

    for copy in weights:
        copy.wait()

    def across(kind, c, src, dst, side):
        return pltpu.make_async_remote_copy(
            src_ref=src,
            dst_ref=dst,
            send_sem=x_send.at[kind, c],
            recv_sem=x_recv.at[kind, c],
            device_id={"rep": side},
            device_id_type=MESH,
        )

    def far(c):
        return (
            across(0, c, part16.at[0, c, opp], far_in.at[0, c], right),
            across(1, c, part16.at[1, c, opp], far_in.at[1, c], left),
        )

    def near(c):
        return (
            across(2, c, part16.at[1, c, right], near_in.at[1, c], right),
            across(3, c, part16.at[0, c, left], near_in.at[0, c], left),
        )

    def relayed(c):
        return (
            across(4, c, relay.at[0, c], relay_in.at[0, c], right),
            across(5, c, relay.at[1, c], relay_in.at[1, c], left),
        )

    def hidden_out(c):
        return (
            across(6, c, hid.at[c, rep], hid.at[c, rep], right),
            across(7, c, hid.at[c, rep], hid.at[c, rep], left),
        )

    def hidden_in(c):
        return (
            across(6, c, hid.at[c, left], hid.at[c, left], right),
            across(7, c, hid.at[c, right], hid.at[c, right], left),
        )

    def onward(c):
        return (
            across(8, c, hid.at[c, left, :, pl.ds(0, half)], hid.at[c, left, :, pl.ds(0, half)], right),
            across(9, c, hid.at[c, right, :, pl.ds(half, half)], hid.at[c, right, :, pl.ds(half, half)], left),
        )

    def onward_in(c):
        return (
            across(8, c, hid.at[c, opp, :, pl.ds(0, half)], hid.at[c, opp, :, pl.ds(0, half)], right),
            across(9, c, hid.at[c, opp, :, pl.ds(half, half)], hid.at[c, opp, :, pl.ds(half, half)], left),
        )

    def start(copies):
        for copy in copies:
            copy.start()

    def arrive(copies):
        for copy in copies:
            copy.wait_recv()

    def multiply(c):
        group = recv.at[pl.ds(c * SPAN, SPAN)]
        pltpu.make_async_copy(group, group, recv_sem.at[c]).wait()
        tiles = unpack(recv, c)
        x = jnp.concatenate(
            [
                jnp.concatenate(
                    [tiles[64 * b : 64 * b + 64, LANES * q : LANES * (q + 1)] for b in range(BLOCKS)],
                    axis=1,
                )
                for q in range(QUADS)
            ],
            axis=0,
        )
        for side, w in enumerate((wg, wu)):
            product = dot_t(x, w[...])
            for owner in range(n_rep):
                share = product[quarter * owner : quarter * (owner + 1)]
                part[side, c, owner] = share
                part16[side, c, owner] = share.astype(BF16)
        start(far(c))
        start(near(c))

    def add_on(c):
        arrive(far(c))
        relay[0, c] = (part[0, c, right] + far_in[0, c].astype(F32)).astype(BF16)
        relay[1, c] = (part[1, c, left] + far_in[1, c].astype(F32)).astype(BF16)
        start(relayed(c))

    def activate(c):
        arrive(near(c))
        arrive(relayed(c))
        gate = part[0, c, rep] + near_in[0, c].astype(F32) + relay_in[0, c].astype(F32)
        up = part[1, c, rep] + near_in[1, c].astype(F32) + relay_in[1, c].astype(F32)
        hid[c, rep] = (gate / (1.0 + jnp.exp(-gate)) * up).astype(BF16)
        start(hidden_out(c))

    def forward(c):
        arrive(hidden_in(c))
        start(onward(c))

    def down(c):
        arrive(onward_in(c))
        rows2d = dot(hid[c].reshape(n_rep * quarter, ff), wd[...]).astype(BF16)
        pack(rows2d, back, c)

        deliver(c, -1, behind, back, home, back_sem, home_sem)

    @pl.loop(0, n_z + STAGES - 1)
    def _(i):
        for age, stage in ((4, down), (3, forward), (2, activate), (1, add_on), (0, multiply)):

            @pl.when((i >= age) & (i < n_z + age))
            def _(age=age, stage=stage):
                stage(i - age)

    @pl.loop(0, n_z)
    def _(c):
        group = home.at[pl.ds(c * SPAN, SPAN)]
        pltpu.make_async_copy(group, group, home_sem.at[c]).wait()
        tiles = unpack(home, c)
        for q in range(QUADS):
            for s in range(4):
                for b in range(BLOCKS):
                    table[
                        pl.ds((4 * q + s) * experts + c * SPAN, SPAN), LANES * b : LANES * (b + 1)
                    ] = tiles[64 * b + 16 * s : 64 * b + 16 * s + 16, LANES * q : LANES * (q + 1)]

    slot, prob = slot_t[...].T, prob_t[...].T
    mix = jnp.concatenate(
        [jnp.where(slot == float(s), prob, 0.0) for s in range(CAP)], axis=1
    )
    high = mix.astype(BF16)
    low = (mix - high.astype(F32)).astype(BF16)
    out[...] = (dot(high, table[...]) + dot(low, table[...])).astype(BF16)

    sent = send.at[pl.ds(1, experts - 1)]
    pltpu.make_async_copy(sent, sent, send_sem).wait()
    returned = back.at[pl.ds(1, experts - 1)]
    pltpu.make_async_copy(returned, returned, back_sem).wait()

    @pl.loop(0, n_z)
    def _(c):
        for copies in (far(c), near(c), relayed(c), hidden_out(c), onward(c)):
            for copy in copies:
                copy.wait_send()


def local(sizes, tokens, expert_ids, route_weights, w_gate, w_up, w_down):
    n_z, n_y, n_rep = sizes
    experts = n_z * SPAN
    rows, width = tokens.shape
    ff = w_gate.shape[1]
    quarter = SPAN * CAP // n_rep
    messages = pltpu.VMEM((experts, QUADS, SPAN, LANES), BF16)
    pair = pltpu.VMEM((2, n_z, quarter, ff), BF16)
    vmem = pl.BlockSpec(memory_space=pltpu.VMEM)
    anywhere = pl.BlockSpec(memory_space=pl.ANY)
    return pl.pallas_call(
        functools.partial(kernel, sizes),
        out_shape=jax.ShapeDtypeStruct((rows, width), BF16),
        in_specs=[vmem] * 3 + [anywhere] * 3,
        out_specs=vmem,
        scratch_shapes=[
            pltpu.VMEM((ff, width), BF16),
            pltpu.VMEM((ff, width), BF16),
            pltpu.VMEM((ff, width), BF16),
            pltpu.VMEM((256, 256), BF16),
            pltpu.VMEM((256, 256), BF16),
            pltpu.VMEM((experts, rows), F32),
            pltpu.VMEM((experts, rows), F32),
            messages,
            messages,
            messages,
            messages,
            pltpu.VMEM((CAP * experts, width), BF16),
            pltpu.VMEM((2, n_z, n_rep, quarter, ff), F32),
            pltpu.VMEM((2, n_z, n_rep, quarter, ff), BF16),
            pair,
            pair,
            pair,
            pair,
            pltpu.VMEM((n_z, n_rep, quarter, ff), BF16),
            pltpu.SemaphoreType.DMA((3,)),
            pltpu.SemaphoreType.DMA,
            pltpu.SemaphoreType.DMA((n_z,)),
            pltpu.SemaphoreType.DMA,
            pltpu.SemaphoreType.DMA((n_z,)),
            pltpu.SemaphoreType.DMA((10, n_z)),
            pltpu.SemaphoreType.DMA((10, n_z)),
        ],
        compiler_params=pltpu.CompilerParams(
            collective_id=0, has_side_effects=True, vmem_limit_bytes=58 * 1024 * 1024
        ),
    )(tokens, expert_ids.T, route_weights.T, w_gate, w_up, w_down)


def solution(mesh):
    n_rep, experts = mesh.shape["rep"], mesh.shape["exp"]
    sizes = (experts // SPAN, SPAN // CORES, n_rep)
    return jax.shard_map(
        functools.partial(local, sizes),
        mesh=mesh,
        in_specs=(
            P("exp", "rep"),
            P("exp", None),
            P("exp", None),
            P("exp", None, "rep"),
            P("exp", None, "rep"),
            P("exp", None, "rep"),
        ),
        out_specs=P("exp", "rep"),
        check_vma=False,
    )
```

```python
import functools

import jax
import jax.numpy as jnp
from jax import lax
from jax.experimental import pallas as pl
from jax.experimental.pallas import tpu as pltpu
from jax.sharding import PartitionSpec as P

MESH = pl.DeviceIdType.MESH
BF16 = jnp.bfloat16
F32 = jnp.float32
CAP = 12
QUADS = 3
SPAN = 16
LANES = 128
BLOCKS = 4
CORES = 2
STAGES = 5


def dot(a, b):
    return jnp.dot(a, b, preferred_element_type=F32)


def dot_t(a, b):
    return lax.dot_general(a, b, (((1,), (1,)), ((), ())), preferred_element_type=F32)


def kernel(
    sizes,
    tok,
    ids,
    route,
    wg_any,
    wu_any,
    wd_any,
    out,
    wg,
    wu,
    wd,
    perm,
    perm_t,
    slot_t,
    prob_t,
    send,
    recv,
    back,
    home,
    table,
    part,
    part16,
    far_in,
    near_in,
    relay,
    relay_in,
    hid,
    w_sem,
    send_sem,
    recv_sem,
    back_sem,
    home_sem,
    x_send,
    x_recv,
):
    n_z, n_y, n_rep = sizes
    experts = n_z * SPAN
    ff = wg.shape[0]
    half = ff // 2
    quarter = SPAN * CAP // n_rep
    me, rep = lax.axis_index("exp"), lax.axis_index("rep")
    my_z, my_y, my_c = lax.div(me, SPAN), lax.rem(lax.div(me, CORES), n_y), lax.rem(me, CORES)
    right, left, opp = (lax.rem(rep + step, n_rep) for step in (1, n_rep - 1, 2))

    def spots(sign):
        return [
            lax.rem(my_y + n_y + sign * (h // CORES), n_y) * CORES
            + lax.rem(my_c + h % CORES, CORES)
            for h in range(SPAN)
        ]

    ahead, behind = spots(1), spots(-1)
    order = sorted(range(SPAN), key=lambda h: min(h // CORES, n_y - h // CORES))

    def each(g, sign, spot, act):
        planes = [
            lax.rem(my_z + n_y * n_z + sign * (g + i), n_z) * SPAN for i in range(SPAN // CORES)
        ]
        for h in order:
            device = planes[h // CORES] + spot[h]
            if h:
                act(g * SPAN + h, device)
            else:
                pl.when(g > 0)(functools.partial(act, g * SPAN, device))

    barrier = pltpu.get_barrier_semaphore()

    def greet(k, device):
        pl.semaphore_signal(barrier, inc=1, device_id={"exp": device}, device_id_type=MESH)

    @pl.loop(0, n_z)
    def _(g):
        each(g, 1, ahead, greet)

    for side in (left, right):
        pl.semaphore_signal(barrier, inc=1, device_id={"rep": side}, device_id_type=MESH)

    weights = [
        pltpu.make_async_copy(src.at[0], dst, w_sem.at[i])
        for i, (src, dst) in enumerate(((wg_any, wg), (wu_any, wu), (wd_any, wd)))
    ]
    for copy in weights:
        copy.start()

    row = lax.broadcasted_iota(jnp.int32, (256, 256), 0)
    col = lax.broadcasted_iota(jnp.int32, (256, 256), 1)
    perm[...] = (
        col == (row & 3) * 64 + ((row >> 2) & 3) * 16 + (row >> 4)
    ).astype(F32).astype(BF16)
    perm_t[...] = (
        row == (col & 3) * 64 + ((col >> 2) & 3) * 16 + (col >> 4)
    ).astype(F32).astype(BF16)

    chosen = ids[...]
    rows = chosen.shape[1]
    off_z = ((chosen >> 4) - my_z + n_z) & (n_z - 1)
    off_y = (((chosen >> 1) & (n_y - 1)) - my_y + n_y) & (n_y - 1)
    off_c = ((chosen & 1) - my_c + CORES) & 1
    number = ((off_z - off_y) & (n_z - 1)) * SPAN + off_y * CORES + off_c
    probs = route[...] / jnp.sum(route[...], axis=0, keepdims=True)
    place = lax.broadcasted_iota(jnp.int32, (experts, rows), 0)
    named = jnp.zeros((experts, rows), F32)
    prob = jnp.zeros((experts, rows), F32)
    for j in range(chosen.shape[0]):
        hit = number[j : j + 1, :] == place
        named = named + jnp.where(hit, 1.0, 0.0)
        prob = prob + jnp.where(hit, probs[j : j + 1, :], 0.0)
    t_row = lax.broadcasted_iota(jnp.int32, (rows, rows), 0)
    t_col = lax.broadcasted_iota(jnp.int32, (rows, rows), 1)
    earlier = (t_row < t_col).astype(F32).astype(BF16)
    slot_t[...] = jnp.where(named > 0.5, dot(named.astype(BF16), earlier), -1.0)
    prob_t[...] = prob

    pl.semaphore_wait(barrier, experts + 1)

    def deliver(g, sign, spot, src, dst, out_sem, in_sem):
        @pl.when(g == 0)
        def _():
            pltpu.make_async_copy(src.at[0], dst.at[0], in_sem.at[0]).start()

        def go(k, device):
            pltpu.make_async_remote_copy(
                src_ref=src.at[k],
                dst_ref=dst.at[k],
                send_sem=out_sem,
                recv_sem=in_sem.at[g],
                device_id={"exp": device},
                device_id_type=MESH,
            ).start()

        each(g, sign, spot, go)

    def pack(rows2d, place, g):
        stacked = jnp.concatenate(
            [
                jnp.concatenate(
                    [rows2d[64 * q : 64 * q + 64, LANES * b : LANES * (b + 1)] for b in range(BLOCKS)],
                    axis=0,
                )
                for q in range(QUADS)
            ],
            axis=1,
        )
        tiles = dot(perm[...], stacked).astype(BF16)
        for q in range(QUADS):
            place[pl.ds(g * SPAN, SPAN), q] = tiles[:, LANES * q : LANES * (q + 1)].reshape(
                SPAN, SPAN, LANES
            )

    def unpack(place, g):
        tiles = jnp.concatenate(
            [place[pl.ds(g * SPAN, SPAN), q].reshape(256, LANES) for q in range(QUADS)], axis=1
        )
        return dot(perm_t[...], tiles).astype(BF16)

    @pl.loop(0, n_z)
    def _(g):
        slots = slot_t[pl.ds(g * SPAN, SPAN), :]
        onehot = jnp.concatenate(
            [(slots == float(s)).astype(F32).astype(BF16) for s in range(CAP)], axis=0
        )
        pack(dot(onehot, tok[...]).astype(BF16), send, g)

        deliver(g, 1, ahead, send, recv, send_sem, recv_sem)

    for copy in weights:
        copy.wait()

    def across(kind, c, src, dst, side):
        return pltpu.make_async_remote_copy(
            src_ref=src,
            dst_ref=dst,
            send_sem=x_send.at[kind, c],
            recv_sem=x_recv.at[kind, c],
            device_id={"rep": side},
            device_id_type=MESH,
        )

    def far(c):
        return (
            across(0, c, part16.at[0, c, opp], far_in.at[0, c], right),
            across(1, c, part16.at[1, c, opp], far_in.at[1, c], left),
        )

    def near(c):
        return (
            across(2, c, part16.at[1, c, right], near_in.at[1, c], right),
            across(3, c, part16.at[0, c, left], near_in.at[0, c], left),
        )

    def relayed(c):
        return (
            across(4, c, relay.at[0, c], relay_in.at[0, c], right),
            across(5, c, relay.at[1, c], relay_in.at[1, c], left),
        )

    def hidden_out(c):
        return (
            across(6, c, hid.at[c, rep], hid.at[c, rep], right),
            across(7, c, hid.at[c, rep], hid.at[c, rep], left),
        )

    def hidden_in(c):
        return (
            across(6, c, hid.at[c, left], hid.at[c, left], right),
            across(7, c, hid.at[c, right], hid.at[c, right], left),
        )

    def onward(c):
        return (
            across(8, c, hid.at[c, left, :, pl.ds(0, half)], hid.at[c, left, :, pl.ds(0, half)], right),
            across(9, c, hid.at[c, right, :, pl.ds(half, half)], hid.at[c, right, :, pl.ds(half, half)], left),
        )

    def onward_in(c):
        return (
            across(8, c, hid.at[c, opp, :, pl.ds(0, half)], hid.at[c, opp, :, pl.ds(0, half)], right),
            across(9, c, hid.at[c, opp, :, pl.ds(half, half)], hid.at[c, opp, :, pl.ds(half, half)], left),
        )

    def start(copies):
        for copy in copies:
            copy.start()

    def arrive(copies):
        for copy in copies:
            copy.wait_recv()

    def multiply(c):
        group = recv.at[pl.ds(c * SPAN, SPAN)]
        pltpu.make_async_copy(group, group, recv_sem.at[c]).wait()
        tiles = unpack(recv, c)
        x = jnp.concatenate(
            [
                jnp.concatenate(
                    [tiles[64 * b : 64 * b + 64, LANES * q : LANES * (q + 1)] for b in range(BLOCKS)],
                    axis=1,
                )
                for q in range(QUADS)
            ],
            axis=0,
        )
        for side, w in enumerate((wg, wu)):
            product = dot_t(x, w[...])
            for owner in range(n_rep):
                share = product[quarter * owner : quarter * (owner + 1)]
                part[side, c, owner] = share
                part16[side, c, owner] = share.astype(BF16)
        start(far(c))
        start(near(c))

    def add_on(c):
        arrive(far(c))
        relay[0, c] = (part[0, c, right] + far_in[0, c].astype(F32)).astype(BF16)
        relay[1, c] = (part[1, c, left] + far_in[1, c].astype(F32)).astype(BF16)
        start(relayed(c))

    def activate(c):
        arrive(near(c))
        arrive(relayed(c))
        gate = part[0, c, rep] + near_in[0, c].astype(F32) + relay_in[0, c].astype(F32)
        up = part[1, c, rep] + near_in[1, c].astype(F32) + relay_in[1, c].astype(F32)
        hid[c, rep] = (gate / (1.0 + jnp.exp(-gate)) * up).astype(BF16)
        start(hidden_out(c))

    def forward(c):
        arrive(hidden_in(c))
        start(onward(c))

    def down(c):
        arrive(onward_in(c))
        rows2d = dot(hid[c].reshape(n_rep * quarter, ff), wd[...]).astype(BF16)
        pack(rows2d, back, c)

        deliver(c, -1, behind, back, home, back_sem, home_sem)

    @pl.loop(0, n_z + STAGES - 1)
    def _(i):
        for age, stage in ((4, down), (3, forward), (2, activate), (1, add_on), (0, multiply)):

            @pl.when((i >= age) & (i < n_z + age))
            def _(age=age, stage=stage):
                stage(i - age)

    @pl.loop(0, n_z)
    def _(c):
        group = home.at[pl.ds(c * SPAN, SPAN)]
        pltpu.make_async_copy(group, group, home_sem.at[c]).wait()
        tiles = unpack(home, c)
        for q in range(QUADS):
            for s in range(4):
                for b in range(BLOCKS):
                    table[
                        pl.ds((4 * q + s) * experts + c * SPAN, SPAN), LANES * b : LANES * (b + 1)
                    ] = tiles[64 * b + 16 * s : 64 * b + 16 * s + 16, LANES * q : LANES * (q + 1)]

    slot, prob = slot_t[...].T, prob_t[...].T
    mix = jnp.concatenate(
        [jnp.where(slot == float(s), prob, 0.0) for s in range(CAP)], axis=1
    )
    high = mix.astype(BF16)
    low = (mix - high.astype(F32)).astype(BF16)
    out[...] = (dot(high, table[...]) + dot(low, table[...])).astype(BF16)

    sent = send.at[pl.ds(1, experts - 1)]
    pltpu.make_async_copy(sent, sent, send_sem).wait()
    returned = back.at[pl.ds(1, experts - 1)]
    pltpu.make_async_copy(returned, returned, back_sem).wait()

    @pl.loop(0, n_z)
    def _(c):
        for copies in (far(c), near(c), relayed(c), hidden_out(c), onward(c)):
            for copy in copies:
                copy.wait_send()


def local(sizes, tokens, expert_ids, route_weights, w_gate, w_up, w_down):
    n_z, n_y, n_rep = sizes
    experts = n_z * SPAN
    rows, width = tokens.shape
    ff = w_gate.shape[1]
    quarter = SPAN * CAP // n_rep
    messages = pltpu.VMEM((experts, QUADS, SPAN, LANES), BF16)
    pair = pltpu.VMEM((2, n_z, quarter, ff), BF16)
    vmem = pl.BlockSpec(memory_space=pltpu.VMEM)
    anywhere = pl.BlockSpec(memory_space=pl.ANY)
    return pl.pallas_call(
        functools.partial(kernel, sizes),
        out_shape=jax.ShapeDtypeStruct((rows, width), BF16),
        in_specs=[vmem] * 3 + [anywhere] * 3,
        out_specs=vmem,
        scratch_shapes=[
            pltpu.VMEM((ff, width), BF16),
            pltpu.VMEM((ff, width), BF16),
            pltpu.VMEM((ff, width), BF16),
            pltpu.VMEM((256, 256), BF16),
            pltpu.VMEM((256, 256), BF16),
            pltpu.VMEM((experts, rows), F32),
            pltpu.VMEM((experts, rows), F32),
            messages,
            messages,
            messages,
            messages,
            pltpu.VMEM((CAP * experts, width), BF16),
            pltpu.VMEM((2, n_z, n_rep, quarter, ff), F32),
            pltpu.VMEM((2, n_z, n_rep, quarter, ff), BF16),
            pair,
            pair,
            pair,
            pair,
            pltpu.VMEM((n_z, n_rep, quarter, ff), BF16),
            pltpu.SemaphoreType.DMA((3,)),
            pltpu.SemaphoreType.DMA,
            pltpu.SemaphoreType.DMA((n_z,)),
            pltpu.SemaphoreType.DMA,
            pltpu.SemaphoreType.DMA((n_z,)),
            pltpu.SemaphoreType.DMA((10, n_z)),
            pltpu.SemaphoreType.DMA((10, n_z)),
        ],
        compiler_params=pltpu.CompilerParams(
            collective_id=0, has_side_effects=True, vmem_limit_bytes=58 * 1024 * 1024
        ),
    )(tokens, expert_ids.T, route_weights.T, w_gate, w_up, w_down)


def solution(mesh):
    n_rep, experts = mesh.shape["rep"], mesh.shape["exp"]
    sizes = (experts // SPAN, SPAN // CORES, n_rep)
    return jax.shard_map(
        functools.partial(local, sizes),
        mesh=mesh,
        in_specs=(
            P("exp", "rep"),
            P("exp", None),
            P("exp", None),
            P("exp", None, "rep"),
            P("exp", None, "rep"),
            P("exp", None, "rep"),
        ),
        out_specs=P("exp", "rep"),
        check_vma=False,
    )
```

```python
import functools

import jax
import jax.numpy as jnp
from jax import lax
from jax.experimental import pallas as pl
from jax.experimental.pallas import tpu as pltpu
from jax.sharding import PartitionSpec as P

MESH = pl.DeviceIdType.MESH
BF16 = jnp.bfloat16
F32 = jnp.float32
CAP = 12
QUADS = 3
SPAN = 16
LANES = 128
BLOCKS = 4
CORES = 2
STAGES = 5
PLANES = {8: (0, 1, 2, 6, 4, 3, 5, 7), 2: (0, 1), 1: (0,)}


def dot(a, b):
    return jnp.dot(a, b, preferred_element_type=F32)


def dot_t(a, b):
    return lax.dot_general(a, b, (((1,), (1,)), ((), ())), preferred_element_type=F32)


def kernel(
    sizes,
    tok,
    ids,
    route,
    wg_any,
    wu_any,
    wd_any,
    out,
    wg,
    wu,
    wd,
    perm,
    perm_t,
    slot_t,
    prob_t,
    send,
    recv,
    back,
    home,
    table,
    part,
    part16,
    far_in,
    near_in,
    relay,
    relay_in,
    hid,
    w_sem,
    send_sem,
    recv_sem,
    back_sem,
    home_sem,
    x_send,
    x_recv,
):
    n_z, n_y, n_rep = sizes
    experts = n_z * SPAN
    ff = wg.shape[0]
    half = ff // 2
    quarter = SPAN * CAP // n_rep
    me, rep = lax.axis_index("exp"), lax.axis_index("rep")
    my_z, my_y, my_c = lax.div(me, SPAN), lax.rem(lax.div(me, CORES), n_y), lax.rem(me, CORES)
    right, left, opp = (lax.rem(rep + step, n_rep) for step in (1, n_rep - 1, 2))

    def spots(sign):
        return [
            lax.rem(my_y + n_y + sign * (h // CORES), n_y) * CORES
            + lax.rem(my_c + h % CORES, CORES)
            for h in range(SPAN)
        ]

    ahead, behind = spots(1), spots(-1)
    order = sorted(range(SPAN), key=lambda h: min(h // CORES, n_y - h // CORES))

    def each(v, sign, spot, act):
        base = lax.rem(my_z + n_z + sign * PLANES[n_z][v], n_z) * SPAN
        for h in order:
            if v or h:
                act(v * SPAN + h, base + spot[h])

    barrier = pltpu.get_barrier_semaphore()

    def greet(k, device):
        pl.semaphore_signal(barrier, inc=1, device_id={"exp": device}, device_id_type=MESH)

    for v in range(n_z):
        each(v, 1, ahead, greet)

    for side in (left, right):
        pl.semaphore_signal(barrier, inc=1, device_id={"rep": side}, device_id_type=MESH)

    weights = [
        pltpu.make_async_copy(src.at[0], dst, w_sem.at[i])
        for i, (src, dst) in enumerate(((wg_any, wg), (wu_any, wu), (wd_any, wd)))
    ]
    for copy in weights:
        copy.start()

    row = lax.broadcasted_iota(jnp.int32, (256, 256), 0)
    col = lax.broadcasted_iota(jnp.int32, (256, 256), 1)
    perm[...] = (
        col == (row & 3) * 64 + ((row >> 2) & 3) * 16 + (row >> 4)
    ).astype(F32).astype(BF16)
    perm_t[...] = (
        row == (col & 3) * 64 + ((col >> 2) & 3) * 16 + (col >> 4)
    ).astype(F32).astype(BF16)

    chosen = ids[...]
    rows = chosen.shape[1]
    off_z = ((chosen >> 4) - my_z + n_z) & (n_z - 1)
    off_y = (((chosen >> 1) & (n_y - 1)) - my_y + n_y) & (n_y - 1)
    off_c = ((chosen & 1) - my_c + CORES) & 1
    turn = sum(jnp.where(off_z == offset, v, 0) for v, offset in enumerate(PLANES[n_z]))
    number = turn * SPAN + off_y * CORES + off_c
    probs = route[...] / jnp.sum(route[...], axis=0, keepdims=True)
    place = lax.broadcasted_iota(jnp.int32, (experts, rows), 0)
    named = jnp.zeros((experts, rows), F32)
    prob = jnp.zeros((experts, rows), F32)
    for j in range(chosen.shape[0]):
        hit = number[j : j + 1, :] == place
        named = named + jnp.where(hit, 1.0, 0.0)
        prob = prob + jnp.where(hit, probs[j : j + 1, :], 0.0)
    t_row = lax.broadcasted_iota(jnp.int32, (rows, rows), 0)
    t_col = lax.broadcasted_iota(jnp.int32, (rows, rows), 1)
    earlier = (t_row < t_col).astype(F32).astype(BF16)
    slot_t[...] = jnp.where(named > 0.5, dot(named.astype(BF16), earlier), -1.0)
    prob_t[...] = prob

    pl.semaphore_wait(barrier, experts + 1)

    def deliver(v, sign, spot, src, dst, out_sem, in_sem):
        if v == 0:
            pltpu.make_async_copy(src.at[0], dst.at[0], in_sem.at[0]).start()

        def go(k, device):
            pltpu.make_async_remote_copy(
                src_ref=src.at[k],
                dst_ref=dst.at[k],
                send_sem=out_sem,
                recv_sem=in_sem.at[v],
                device_id={"exp": device},
                device_id_type=MESH,
            ).start()

        each(v, sign, spot, go)

    def pack(rows2d, place, g):
        stacked = jnp.concatenate(
            [
                jnp.concatenate(
                    [rows2d[64 * q : 64 * q + 64, LANES * b : LANES * (b + 1)] for b in range(BLOCKS)],
                    axis=0,
                )
                for q in range(QUADS)
            ],
            axis=1,
        )
        tiles = dot(perm[...], stacked).astype(BF16)
        for q in range(QUADS):
            place[pl.ds(g * SPAN, SPAN), q] = tiles[:, LANES * q : LANES * (q + 1)].reshape(
                SPAN, SPAN, LANES
            )

    def unpack(place, g):
        tiles = jnp.concatenate(
            [place[pl.ds(g * SPAN, SPAN), q].reshape(256, LANES) for q in range(QUADS)], axis=1
        )
        return dot(perm_t[...], tiles).astype(BF16)

    for g in range(n_z):
        slots = slot_t[pl.ds(g * SPAN, SPAN), :]
        onehot = jnp.concatenate(
            [(slots == float(s)).astype(F32).astype(BF16) for s in range(CAP)], axis=0
        )
        pack(dot(onehot, tok[...]).astype(BF16), send, g)

        deliver(g, 1, ahead, send, recv, send_sem, recv_sem)

    for copy in weights:
        copy.wait()

    def across(kind, c, src, dst, side):
        return pltpu.make_async_remote_copy(
            src_ref=src,
            dst_ref=dst,
            send_sem=x_send.at[kind, c],
            recv_sem=x_recv.at[kind, c],
            device_id={"rep": side},
            device_id_type=MESH,
        )

    def far(c):
        return (
            across(0, c, part16.at[0, c, opp], far_in.at[0, c], right),
            across(1, c, part16.at[1, c, opp], far_in.at[1, c], left),
        )

    def near(c):
        return (
            across(2, c, part16.at[1, c, right], near_in.at[1, c], right),
            across(3, c, part16.at[0, c, left], near_in.at[0, c], left),
        )

    def relayed(c):
        return (
            across(4, c, relay.at[0, c], relay_in.at[0, c], right),
            across(5, c, relay.at[1, c], relay_in.at[1, c], left),
        )

    def hidden_out(c):
        return (
            across(6, c, hid.at[c, rep], hid.at[c, rep], right),
            across(7, c, hid.at[c, rep], hid.at[c, rep], left),
        )

    def hidden_in(c):
        return (
            across(6, c, hid.at[c, left], hid.at[c, left], right),
            across(7, c, hid.at[c, right], hid.at[c, right], left),
        )

    def onward(c):
        return (
            across(8, c, hid.at[c, left, :, pl.ds(0, half)], hid.at[c, left, :, pl.ds(0, half)], right),
            across(9, c, hid.at[c, right, :, pl.ds(half, half)], hid.at[c, right, :, pl.ds(half, half)], left),
        )

    def onward_in(c):
        return (
            across(8, c, hid.at[c, opp, :, pl.ds(0, half)], hid.at[c, opp, :, pl.ds(0, half)], right),
            across(9, c, hid.at[c, opp, :, pl.ds(half, half)], hid.at[c, opp, :, pl.ds(half, half)], left),
        )

    def start(copies):
        for copy in copies:
            copy.start()

    def arrive(copies):
        for copy in copies:
            copy.wait_recv()

    def multiply(c):
        group = recv.at[pl.ds(c * SPAN, SPAN)]
        pltpu.make_async_copy(group, group, recv_sem.at[c]).wait()
        tiles = unpack(recv, c)
        x = jnp.concatenate(
            [
                jnp.concatenate(
                    [tiles[64 * b : 64 * b + 64, LANES * q : LANES * (q + 1)] for b in range(BLOCKS)],
                    axis=1,
                )
                for q in range(QUADS)
            ],
            axis=0,
        )
        for side, w in enumerate((wg, wu)):
            product = dot_t(x, w[...])
            for owner in range(n_rep):
                share = product[quarter * owner : quarter * (owner + 1)]
                part[side, c, owner] = share
                part16[side, c, owner] = share.astype(BF16)
        start(far(c))
        start(near(c))

    def add_on(c):
        arrive(far(c))
        relay[0, c] = (part[0, c, right] + far_in[0, c].astype(F32)).astype(BF16)
        relay[1, c] = (part[1, c, left] + far_in[1, c].astype(F32)).astype(BF16)
        start(relayed(c))

    def activate(c):
        arrive(near(c))
        arrive(relayed(c))
        gate = part[0, c, rep] + near_in[0, c].astype(F32) + relay_in[0, c].astype(F32)
        up = part[1, c, rep] + near_in[1, c].astype(F32) + relay_in[1, c].astype(F32)
        hid[c, rep] = (gate / (1.0 + jnp.exp(-gate)) * up).astype(BF16)
        start(hidden_out(c))

    def forward(c):
        arrive(hidden_in(c))
        start(onward(c))

    def down(c):
        arrive(onward_in(c))
        rows2d = dot(hid[c].reshape(n_rep * quarter, ff), wd[...]).astype(BF16)
        pack(rows2d, back, c)

        for v in range(n_z):

            @pl.when(c == v)
            def _(v=v):
                deliver(v, -1, behind, back, home, back_sem, home_sem)

    @pl.loop(0, n_z + STAGES - 1)
    def _(i):
        for age, stage in ((4, down), (3, forward), (2, activate), (1, add_on), (0, multiply)):

            @pl.when((i >= age) & (i < n_z + age))
            def _(age=age, stage=stage):
                stage(i - age)

    slot, prob = slot_t[...].T, prob_t[...].T
    mix = jnp.concatenate(
        [jnp.where(slot == float(s), prob, 0.0) for s in range(CAP)], axis=1
    )
    high = mix.astype(BF16)
    low = (mix - high.astype(F32)).astype(BF16)
    @pl.loop(0, n_z)
    def _(c):
        group = home.at[pl.ds(c * SPAN, SPAN)]
        pltpu.make_async_copy(group, group, home_sem.at[c]).wait()
        tiles = unpack(home, c)
        for q in range(QUADS):
            for s in range(4):
                for b in range(BLOCKS):
                    table[
                        pl.ds((4 * q + s) * experts + c * SPAN, SPAN), LANES * b : LANES * (b + 1)
                    ] = tiles[64 * b + 16 * s : 64 * b + 16 * s + 16, LANES * q : LANES * (q + 1)]

    out[...] = (dot(high, table[...]) + dot(low, table[...])).astype(BF16)

    sent = send.at[pl.ds(1, experts - 1)]
    pltpu.make_async_copy(sent, sent, send_sem).wait()
    returned = back.at[pl.ds(1, experts - 1)]
    pltpu.make_async_copy(returned, returned, back_sem).wait()

    @pl.loop(0, n_z)
    def _(c):
        for copies in (far(c), near(c), relayed(c), hidden_out(c), onward(c)):
            for copy in copies:
                copy.wait_send()


def local(sizes, tokens, expert_ids, route_weights, w_gate, w_up, w_down):
    n_z, n_y, n_rep = sizes
    experts = n_z * SPAN
    rows, width = tokens.shape
    ff = w_gate.shape[1]
    quarter = SPAN * CAP // n_rep
    messages = pltpu.VMEM((experts, QUADS, SPAN, LANES), BF16)
    pair = pltpu.VMEM((2, n_z, quarter, ff), BF16)
    vmem = pl.BlockSpec(memory_space=pltpu.VMEM)
    anywhere = pl.BlockSpec(memory_space=pl.ANY)
    return pl.pallas_call(
        functools.partial(kernel, sizes),
        out_shape=jax.ShapeDtypeStruct((rows, width), BF16),
        in_specs=[vmem] * 3 + [anywhere] * 3,
        out_specs=vmem,
        scratch_shapes=[
            pltpu.VMEM((ff, width), BF16),
            pltpu.VMEM((ff, width), BF16),
            pltpu.VMEM((ff, width), BF16),
            pltpu.VMEM((256, 256), BF16),
            pltpu.VMEM((256, 256), BF16),
            pltpu.VMEM((experts, rows), F32),
            pltpu.VMEM((experts, rows), F32),
            messages,
            messages,
            messages,
            messages,
            pltpu.VMEM((CAP * experts, width), BF16),
            pltpu.VMEM((2, n_z, n_rep, quarter, ff), F32),
            pltpu.VMEM((2, n_z, n_rep, quarter, ff), BF16),
            pair,
            pair,
            pair,
            pair,
            pltpu.VMEM((n_z, n_rep, quarter, ff), BF16),
            pltpu.SemaphoreType.DMA((3,)),
            pltpu.SemaphoreType.DMA,
            pltpu.SemaphoreType.DMA((n_z,)),
            pltpu.SemaphoreType.DMA,
            pltpu.SemaphoreType.DMA((n_z,)),
            pltpu.SemaphoreType.DMA((10, n_z)),
            pltpu.SemaphoreType.DMA((10, n_z)),
        ],
        compiler_params=pltpu.CompilerParams(
            collective_id=0, has_side_effects=True, vmem_limit_bytes=58 * 1024 * 1024
        ),
    )(tokens, expert_ids.T, route_weights.T, w_gate, w_up, w_down)


def solution(mesh):
    n_rep, experts = mesh.shape["rep"], mesh.shape["exp"]
    sizes = (experts // SPAN, SPAN // CORES, n_rep)
    return jax.shard_map(
        functools.partial(local, sizes),
        mesh=mesh,
        in_specs=(
            P("exp", "rep"),
            P("exp", None),
            P("exp", None),
            P("exp", None, "rep"),
            P("exp", None, "rep"),
            P("exp", None, "rep"),
        ),
        out_specs=P("exp", "rep"),
        check_vma=False,
    )
```

```python
import functools

import jax
import jax.numpy as jnp
from jax import lax
from jax.experimental import pallas as pl
from jax.experimental.pallas import tpu as pltpu
from jax.sharding import PartitionSpec as P

MESH = pl.DeviceIdType.MESH
BF16 = jnp.bfloat16
F32 = jnp.float32
CAP = 12
QUADS = 3
SPAN = 16
LANES = 128
BLOCKS = 4
CORES = 2
STAGES = 5


def dot(a, b):
    return jnp.dot(a, b, preferred_element_type=F32)


def dot_t(a, b):
    return lax.dot_general(a, b, (((1,), (1,)), ((), ())), preferred_element_type=F32)


def kernel(
    sizes,
    tok,
    ids,
    route,
    wg_any,
    wu_any,
    wd_any,
    out,
    wg,
    wu,
    wd,
    perm,
    perm_t,
    slot_t,
    prob_t,
    send,
    recv,
    back,
    home,
    table,
    part,
    part16,
    far_in,
    near_in,
    relay,
    relay_in,
    hid,
    w_sem,
    send_sem,
    recv_sem,
    back_sem,
    home_sem,
    x_send,
    x_recv,
):
    n_z, n_y, n_rep = sizes
    experts = n_z * SPAN
    ff = wg.shape[0]
    half = ff // 2
    quarter = SPAN * CAP // n_rep
    me, rep = lax.axis_index("exp"), lax.axis_index("rep")
    my_z, my_y, my_c = lax.div(me, SPAN), lax.rem(lax.div(me, CORES), n_y), lax.rem(me, CORES)
    right, left, opp = (lax.rem(rep + step, n_rep) for step in (1, n_rep - 1, 2))

    def spots(sign):
        return [
            lax.rem(my_y + n_y + sign * (h // CORES), n_y) * CORES
            + lax.rem(my_c + h % CORES, CORES)
            for h in range(SPAN)
        ]

    ahead, behind = spots(1), spots(-1)
    planes = {
        sign: [lax.rem(my_z + n_z + sign * offset, n_z) * SPAN for offset in range(n_z)]
        for sign in (1, -1)
    }

    def each(v, sign, spot, act):
        for h in sorted(range(SPAN), key=lambda h: ((h // 2) * 3 + (h % 2) * 4) % 8 * 2 + h % 2):
            if v or h:
                act(v * SPAN + h, planes[sign][(h // CORES + v) % n_z] + spot[h])

    barrier = pltpu.get_barrier_semaphore()

    def greet(k, device):
        pl.semaphore_signal(barrier, inc=1, device_id={"exp": device}, device_id_type=MESH)

    for v in range(n_z):
        each(v, 1, ahead, greet)

    for side in (left, right):
        pl.semaphore_signal(barrier, inc=1, device_id={"rep": side}, device_id_type=MESH)

    weights = [
        pltpu.make_async_copy(src.at[0], dst, w_sem.at[i])
        for i, (src, dst) in enumerate(((wg_any, wg), (wu_any, wu), (wd_any, wd)))
    ]
    for copy in weights:
        copy.start()

    row = lax.broadcasted_iota(jnp.int32, (256, 256), 0)
    col = lax.broadcasted_iota(jnp.int32, (256, 256), 1)
    perm[...] = (
        col == (row & 3) * 64 + ((row >> 2) & 3) * 16 + (row >> 4)
    ).astype(F32).astype(BF16)
    perm_t[...] = (
        row == (col & 3) * 64 + ((col >> 2) & 3) * 16 + (col >> 4)
    ).astype(F32).astype(BF16)

    chosen = ids[...]
    rows = chosen.shape[1]
    off_z = ((chosen >> 4) - my_z + n_z) & (n_z - 1)
    off_y = (((chosen >> 1) & (n_y - 1)) - my_y + n_y) & (n_y - 1)
    off_c = ((chosen & 1) - my_c + CORES) & 1
    number = ((off_z - off_y) & (n_z - 1)) * SPAN + off_y * CORES + off_c
    probs = route[...] / jnp.sum(route[...], axis=0, keepdims=True)
    place = lax.broadcasted_iota(jnp.int32, (experts, rows), 0)
    named = jnp.zeros((experts, rows), F32)
    prob = jnp.zeros((experts, rows), F32)
    for j in range(chosen.shape[0]):
        hit = number[j : j + 1, :] == place
        named = named + jnp.where(hit, 1.0, 0.0)
        prob = prob + jnp.where(hit, probs[j : j + 1, :], 0.0)
    t_row = lax.broadcasted_iota(jnp.int32, (rows, rows), 0)
    t_col = lax.broadcasted_iota(jnp.int32, (rows, rows), 1)
    earlier = (t_row < t_col).astype(F32).astype(BF16)
    slot_t[...] = jnp.where(named > 0.5, dot(named.astype(BF16), earlier), -1.0)
    prob_t[...] = prob

    pl.semaphore_wait(barrier, experts + 1)

    def deliver(v, sign, spot, src, dst, out_sem, in_sem):
        if v == 0:
            pltpu.make_async_copy(src.at[0], dst.at[0], in_sem.at[0]).start()

        def go(k, device):
            pltpu.make_async_remote_copy(
                src_ref=src.at[k],
                dst_ref=dst.at[k],
                send_sem=out_sem,
                recv_sem=in_sem.at[v],
                device_id={"exp": device},
                device_id_type=MESH,
            ).start()

        each(v, sign, spot, go)

    def pack(rows2d, place, g):
        stacked = jnp.concatenate(
            [
                jnp.concatenate(
                    [rows2d[64 * q : 64 * q + 64, LANES * b : LANES * (b + 1)] for b in range(BLOCKS)],
                    axis=0,
                )
                for q in range(QUADS)
            ],
            axis=1,
        )
        tiles = dot(perm[...], stacked).astype(BF16)
        for q in range(QUADS):
            place[pl.ds(g * SPAN, SPAN), q] = tiles[:, LANES * q : LANES * (q + 1)].reshape(
                SPAN, SPAN, LANES
            )

    def unpack(place, g):
        tiles = jnp.concatenate(
            [place[pl.ds(g * SPAN, SPAN), q].reshape(256, LANES) for q in range(QUADS)], axis=1
        )
        return dot(perm_t[...], tiles).astype(BF16)

    for g in range(n_z):
        slots = slot_t[pl.ds(g * SPAN, SPAN), :]
        onehot = jnp.concatenate(
            [(slots == float(s)).astype(F32).astype(BF16) for s in range(CAP)], axis=0
        )
        pack(dot(onehot, tok[...]).astype(BF16), send, g)

        deliver(g, 1, ahead, send, recv, send_sem, recv_sem)

    for copy in weights:
        copy.wait()

    def across(kind, c, src, dst, side):
        return pltpu.make_async_remote_copy(
            src_ref=src,
            dst_ref=dst,
            send_sem=x_send.at[kind, c],
            recv_sem=x_recv.at[kind, c],
            device_id={"rep": side},
            device_id_type=MESH,
        )

    def far(c):
        return (
            across(0, c, part16.at[0, c, opp], far_in.at[0, c], right),
            across(1, c, part16.at[1, c, opp], far_in.at[1, c], left),
        )

    def near(c):
        return (
            across(2, c, part16.at[1, c, right], near_in.at[1, c], right),
            across(3, c, part16.at[0, c, left], near_in.at[0, c], left),
        )

    def relayed(c):
        return (
            across(4, c, relay.at[0, c], relay_in.at[0, c], right),
            across(5, c, relay.at[1, c], relay_in.at[1, c], left),
        )

    def hidden_out(c):
        return (
            across(6, c, hid.at[c, rep], hid.at[c, rep], right),
            across(7, c, hid.at[c, rep], hid.at[c, rep], left),
        )

    def hidden_in(c):
        return (
            across(6, c, hid.at[c, left], hid.at[c, left], right),
            across(7, c, hid.at[c, right], hid.at[c, right], left),
        )

    def onward(c):
        return (
            across(8, c, hid.at[c, left, :, pl.ds(0, half)], hid.at[c, left, :, pl.ds(0, half)], right),
            across(9, c, hid.at[c, right, :, pl.ds(half, half)], hid.at[c, right, :, pl.ds(half, half)], left),
        )

    def onward_in(c):
        return (
            across(8, c, hid.at[c, opp, :, pl.ds(0, half)], hid.at[c, opp, :, pl.ds(0, half)], right),
            across(9, c, hid.at[c, opp, :, pl.ds(half, half)], hid.at[c, opp, :, pl.ds(half, half)], left),
        )

    def start(copies):
        for copy in copies:
            copy.start()

    def arrive(copies):
        for copy in copies:
            copy.wait_recv()

    def multiply(c):
        group = recv.at[pl.ds(c * SPAN, SPAN)]
        pltpu.make_async_copy(group, group, recv_sem.at[c]).wait()
        tiles = unpack(recv, c)
        x = jnp.concatenate(
            [
                jnp.concatenate(
                    [tiles[64 * b : 64 * b + 64, LANES * q : LANES * (q + 1)] for b in range(BLOCKS)],
                    axis=1,
                )
                for q in range(QUADS)
            ],
            axis=0,
        )
        for side, w in enumerate((wg, wu)):
            product = dot_t(x, w[...])
            for owner in range(n_rep):
                share = product[quarter * owner : quarter * (owner + 1)]
                part[side, c, owner] = share
                part16[side, c, owner] = share.astype(BF16)
        start(far(c))
        start(near(c))

    def add_on(c):
        arrive(far(c))
        relay[0, c] = (part[0, c, right] + far_in[0, c].astype(F32)).astype(BF16)
        relay[1, c] = (part[1, c, left] + far_in[1, c].astype(F32)).astype(BF16)
        start(relayed(c))

    def activate(c):
        arrive(near(c))
        arrive(relayed(c))
        gate = part[0, c, rep] + near_in[0, c].astype(F32) + relay_in[0, c].astype(F32)
        up = part[1, c, rep] + near_in[1, c].astype(F32) + relay_in[1, c].astype(F32)
        hid[c, rep] = (gate / (1.0 + jnp.exp(-gate)) * up).astype(BF16)
        start(hidden_out(c))

    def forward(c):
        arrive(hidden_in(c))
        start(onward(c))

    def down(c):
        arrive(onward_in(c))
        rows2d = dot(hid[c].reshape(n_rep * quarter, ff), wd[...]).astype(BF16)
        pack(rows2d, back, c)

        for v in range(n_z):

            @pl.when(c == v)
            def _(v=v):
                deliver(v, -1, behind, back, home, back_sem, home_sem)

    @pl.loop(0, n_z + STAGES - 1)
    def _(i):
        for age, stage in ((4, down), (3, forward), (2, activate), (1, add_on), (0, multiply)):

            @pl.when((i >= age) & (i < n_z + age))
            def _(age=age, stage=stage):
                stage(i - age)

    slot, prob = slot_t[...].T, prob_t[...].T
    mix = jnp.concatenate(
        [jnp.where(slot == float(s), prob, 0.0) for s in range(CAP)], axis=1
    )
    high = mix.astype(BF16)
    low = (mix - high.astype(F32)).astype(BF16)
    @pl.loop(0, n_z)
    def _(c):
        group = home.at[pl.ds(c * SPAN, SPAN)]
        pltpu.make_async_copy(group, group, home_sem.at[c]).wait()
        tiles = unpack(home, c)
        for q in range(QUADS):
            for s in range(4):
                for b in range(BLOCKS):
                    table[
                        pl.ds((4 * q + s) * experts + c * SPAN, SPAN), LANES * b : LANES * (b + 1)
                    ] = tiles[64 * b + 16 * s : 64 * b + 16 * s + 16, LANES * q : LANES * (q + 1)]

    out[...] = (dot(high, table[...]) + dot(low, table[...])).astype(BF16)

    sent = send.at[pl.ds(1, experts - 1)]
    pltpu.make_async_copy(sent, sent, send_sem).wait()
    returned = back.at[pl.ds(1, experts - 1)]
    pltpu.make_async_copy(returned, returned, back_sem).wait()

    @pl.loop(0, n_z)
    def _(c):
        for copies in (far(c), near(c), relayed(c), hidden_out(c), onward(c)):
            for copy in copies:
                copy.wait_send()


def local(sizes, tokens, expert_ids, route_weights, w_gate, w_up, w_down):
    n_z, n_y, n_rep = sizes
    experts = n_z * SPAN
    rows, width = tokens.shape
    ff = w_gate.shape[1]
    quarter = SPAN * CAP // n_rep
    messages = pltpu.VMEM((experts, QUADS, SPAN, LANES), BF16)
    pair = pltpu.VMEM((2, n_z, quarter, ff), BF16)
    vmem = pl.BlockSpec(memory_space=pltpu.VMEM)
    anywhere = pl.BlockSpec(memory_space=pl.ANY)
    return pl.pallas_call(
        functools.partial(kernel, sizes),
        out_shape=jax.ShapeDtypeStruct((rows, width), BF16),
        in_specs=[vmem] * 3 + [anywhere] * 3,
        out_specs=vmem,
        scratch_shapes=[
            pltpu.VMEM((ff, width), BF16),
            pltpu.VMEM((ff, width), BF16),
            pltpu.VMEM((ff, width), BF16),
            pltpu.VMEM((256, 256), BF16),
            pltpu.VMEM((256, 256), BF16),
            pltpu.VMEM((experts, rows), F32),
            pltpu.VMEM((experts, rows), F32),
            messages,
            messages,
            messages,
            messages,
            pltpu.VMEM((CAP * experts, width), BF16),
            pltpu.VMEM((2, n_z, n_rep, quarter, ff), F32),
            pltpu.VMEM((2, n_z, n_rep, quarter, ff), BF16),
            pair,
            pair,
            pair,
            pair,
            pltpu.VMEM((n_z, n_rep, quarter, ff), BF16),
            pltpu.SemaphoreType.DMA((3,)),
            pltpu.SemaphoreType.DMA,
            pltpu.SemaphoreType.DMA((n_z,)),
            pltpu.SemaphoreType.DMA,
            pltpu.SemaphoreType.DMA((n_z,)),
            pltpu.SemaphoreType.DMA((10, n_z)),
            pltpu.SemaphoreType.DMA((10, n_z)),
        ],
        compiler_params=pltpu.CompilerParams(
            collective_id=0, has_side_effects=True, vmem_limit_bytes=58 * 1024 * 1024
        ),
    )(tokens, expert_ids.T, route_weights.T, w_gate, w_up, w_down)


def solution(mesh):
    n_rep, experts = mesh.shape["rep"], mesh.shape["exp"]
    sizes = (experts // SPAN, SPAN // CORES, n_rep)
    return jax.shard_map(
        functools.partial(local, sizes),
        mesh=mesh,
        in_specs=(
            P("exp", "rep"),
            P("exp", None),
            P("exp", None),
            P("exp", None, "rep"),
            P("exp", None, "rep"),
            P("exp", None, "rep"),
        ),
        out_specs=P("exp", "rep"),
        check_vma=False,
    )
```

```python
import functools

import jax
import jax.numpy as jnp
from jax import lax
from jax.experimental import pallas as pl
from jax.experimental.pallas import tpu as pltpu
from jax.sharding import PartitionSpec as P

MESH = pl.DeviceIdType.MESH
BF16 = jnp.bfloat16
F32 = jnp.float32
CAP = 12
QUADS = 3
SPAN = 16
LANES = 128
BLOCKS = 4
CORES = 2
STAGES = 5


def chunks_of(n_z, n_y):
    if n_z != n_y:
        return [[((i + v) % n_z, i) for i in range(n_y)] for v in range(n_z)]

    def far(offset):
        return min(offset, n_z - offset)

    left = sorted(
        ((z, y) for z in range(n_z) for y in range(n_y)),
        key=lambda p: (far(p[0]) + far(p[1]), abs(far(p[0]) - far(p[1])), p),
    )
    chunks = [[] for _ in range(n_z)]
    chunks[-1], chunks[0] = left[:n_y], left[n_y : 2 * n_y]
    for z, y in reversed(left[2 * n_y :]):

        def cost(chunk):
            along_z = sum(far(p[0]) for p in chunk) + far(z)
            along_y = sum(far(p[1]) for p in chunk) + far(y)
            same = sum((p[0] == z) + (p[1] == y) for p in chunk)
            return along_z**2 + along_y**2 + 40 * same

        open_chunks = [chunk for chunk in chunks[1:-1] if len(chunk) < n_y]
        min(open_chunks, key=cost).append((z, y))
    return [sorted(chunk, key=lambda p: (p[1], p[0])) for chunk in chunks]


def dot(a, b):
    return jnp.dot(a, b, preferred_element_type=F32)


def dot_t(a, b):
    return lax.dot_general(a, b, (((1,), (1,)), ((), ())), preferred_element_type=F32)


def kernel(
    sizes,
    tok,
    ids,
    route,
    wg_any,
    wu_any,
    wd_any,
    out,
    wg,
    wu,
    wd,
    perm,
    perm_t,
    slot_t,
    prob_t,
    send,
    recv,
    back,
    home,
    table,
    part,
    part16,
    far_in,
    near_in,
    relay,
    relay_in,
    hid,
    w_sem,
    send_sem,
    recv_sem,
    back_sem,
    home_sem,
    x_send,
    x_recv,
):
    n_z, n_y, n_rep = sizes
    experts = n_z * SPAN
    ff = wg.shape[0]
    half = ff // 2
    quarter = SPAN * CAP // n_rep
    me, rep = lax.axis_index("exp"), lax.axis_index("rep")
    my_z, my_y, my_c = lax.div(me, SPAN), lax.rem(lax.div(me, CORES), n_y), lax.rem(me, CORES)
    right, left, opp = (lax.rem(rep + step, n_rep) for step in (1, n_rep - 1, 2))

    way = [1 - 2 * my_c, 2 * my_c - 1]

    out_ways, back_ways = [way[0]] * CORES, [-way[0], -way[1]]
    chunks = chunks_of(n_z, n_y)

    def levels(ways):
        return (
            [[lax.rem(my_z + n_z + w * step, n_z) * SPAN for step in range(n_z)] for w in ways],
            [
                [
                    lax.rem(my_y + n_y + w * step, n_y) * CORES + lax.rem(my_c + flip, CORES)
                    for step in range(n_y)
                ]
                for flip, w in enumerate(ways)
            ],
        )

    parts = {1: levels(out_ways), -1: levels(back_ways)}

    def each(v, sign, act):
        in_z, in_y = parts[sign]
        for h in sorted(range(SPAN), key=lambda h: ((h // 2) * 3 + (h % 2) * 4) % 8 * 2 + h % 2):
            (z, y), flip = chunks[v][h // CORES], h % CORES
            if z or y or flip:
                act(v * SPAN + h, in_z[flip][z] + in_y[flip][y])

    barrier = pltpu.get_barrier_semaphore()

    def greet(k, device):
        pl.semaphore_signal(barrier, inc=1, device_id={"exp": device}, device_id_type=MESH)

    for v in range(n_z):
        each(v, 1, greet)

    for side in (left, right):
        pl.semaphore_signal(barrier, inc=1, device_id={"rep": side}, device_id_type=MESH)

    weights = [
        pltpu.make_async_copy(src.at[0], dst, w_sem.at[i])
        for i, (src, dst) in enumerate(((wg_any, wg), (wu_any, wu), (wd_any, wd)))
    ]
    for copy in weights:
        copy.start()

    row = lax.broadcasted_iota(jnp.int32, (256, 256), 0)
    col = lax.broadcasted_iota(jnp.int32, (256, 256), 1)
    perm[...] = (
        col == (row & 3) * 64 + ((row >> 2) & 3) * 16 + (row >> 4)
    ).astype(F32).astype(BF16)
    perm_t[...] = (
        row == (col & 3) * 64 + ((col >> 2) & 3) * 16 + (col >> 4)
    ).astype(F32).astype(BF16)

    chosen = ids[...]
    rows = chosen.shape[1]
    off_z = (way[0] * ((chosen >> 4) - my_z)) & (n_z - 1)
    off_y = (way[0] * (((chosen >> 1) & (n_y - 1)) - my_y)) & (n_y - 1)
    off_c = ((chosen & 1) - my_c + CORES) & 1
    number = off_c
    for v, chunk in enumerate(chunks):
        for i, (z, y) in enumerate(chunk):
            number = number + jnp.where(
                off_z * n_y + off_y == z * n_y + y, v * SPAN + i * CORES, 0
            )
    probs = route[...] / jnp.sum(route[...], axis=0, keepdims=True)
    place = lax.broadcasted_iota(jnp.int32, (experts, rows), 0)
    named = jnp.zeros((experts, rows), F32)
    prob = jnp.zeros((experts, rows), F32)
    for j in range(chosen.shape[0]):
        hit = number[j : j + 1, :] == place
        named = named + jnp.where(hit, 1.0, 0.0)
        prob = prob + jnp.where(hit, probs[j : j + 1, :], 0.0)
    t_row = lax.broadcasted_iota(jnp.int32, (rows, rows), 0)
    t_col = lax.broadcasted_iota(jnp.int32, (rows, rows), 1)
    earlier = (t_row < t_col).astype(F32).astype(BF16)
    slot_t[...] = jnp.where(named > 0.5, dot(named.astype(BF16), earlier), -1.0)
    prob_t[...] = prob

    pl.semaphore_wait(barrier, experts + 1)

    def deliver(v, sign, src, dst, out_sem, in_sem):
        if (0, 0) in chunks[v]:
            own = v * SPAN + CORES * chunks[v].index((0, 0))
            pltpu.make_async_copy(src.at[own], dst.at[own], in_sem.at[v]).start()

        def go(k, device):
            pltpu.make_async_remote_copy(
                src_ref=src.at[k],
                dst_ref=dst.at[k],
                send_sem=out_sem,
                recv_sem=in_sem.at[v],
                device_id={"exp": device},
                device_id_type=MESH,
            ).start()

        each(v, sign, go)

    def pack(rows2d, place, g):
        stacked = jnp.concatenate(
            [
                jnp.concatenate(
                    [rows2d[64 * q : 64 * q + 64, LANES * b : LANES * (b + 1)] for b in range(BLOCKS)],
                    axis=0,
                )
                for q in range(QUADS)
            ],
            axis=1,
        )
        tiles = dot(perm[...], stacked).astype(BF16)
        for q in range(QUADS):
            place[pl.ds(g * SPAN, SPAN), q] = tiles[:, LANES * q : LANES * (q + 1)].reshape(
                SPAN, SPAN, LANES
            )

    def unpack(place, g):
        tiles = jnp.concatenate(
            [place[pl.ds(g * SPAN, SPAN), q].reshape(256, LANES) for q in range(QUADS)], axis=1
        )
        return dot(perm_t[...], tiles).astype(BF16)

    for g in range(n_z):
        slots = slot_t[pl.ds(g * SPAN, SPAN), :]
        onehot = jnp.concatenate(
            [(slots == float(s)).astype(F32).astype(BF16) for s in range(CAP)], axis=0
        )
        pack(dot(onehot, tok[...]).astype(BF16), send, g)

        deliver(g, 1, send, recv, send_sem, recv_sem)

    for copy in weights:
        copy.wait()

    def across(kind, c, src, dst, side):
        return pltpu.make_async_remote_copy(
            src_ref=src,
            dst_ref=dst,
            send_sem=x_send.at[kind, c],
            recv_sem=x_recv.at[kind, c],
            device_id={"rep": side},
            device_id_type=MESH,
        )

    def far(c):
        return (
            across(0, c, part16.at[0, c, opp], far_in.at[0, c], right),
            across(1, c, part16.at[1, c, opp], far_in.at[1, c], left),
        )

    def near(c):
        return (
            across(2, c, part16.at[1, c, right], near_in.at[1, c], right),
            across(3, c, part16.at[0, c, left], near_in.at[0, c], left),
        )

    def relayed(c):
        return (
            across(4, c, relay.at[0, c], relay_in.at[0, c], right),
            across(5, c, relay.at[1, c], relay_in.at[1, c], left),
        )

    def hidden_out(c):
        return (
            across(6, c, hid.at[c, rep], hid.at[c, rep], right),
            across(7, c, hid.at[c, rep], hid.at[c, rep], left),
        )

    def hidden_in(c):
        return (
            across(6, c, hid.at[c, left], hid.at[c, left], right),
            across(7, c, hid.at[c, right], hid.at[c, right], left),
        )

    def onward(c):
        return (
            across(8, c, hid.at[c, left, :, pl.ds(0, half)], hid.at[c, left, :, pl.ds(0, half)], right),
            across(9, c, hid.at[c, right, :, pl.ds(half, half)], hid.at[c, right, :, pl.ds(half, half)], left),
        )

    def onward_in(c):
        return (
            across(8, c, hid.at[c, opp, :, pl.ds(0, half)], hid.at[c, opp, :, pl.ds(0, half)], right),
            across(9, c, hid.at[c, opp, :, pl.ds(half, half)], hid.at[c, opp, :, pl.ds(half, half)], left),
        )

    def start(copies):
        for copy in copies:
            copy.start()

    def arrive(copies):
        for copy in copies:
            copy.wait_recv()

    def multiply(c):
        group = recv.at[pl.ds(c * SPAN, SPAN)]
        pltpu.make_async_copy(group, group, recv_sem.at[c]).wait()
        tiles = unpack(recv, c)
        x = jnp.concatenate(
            [
                jnp.concatenate(
                    [tiles[64 * b : 64 * b + 64, LANES * q : LANES * (q + 1)] for b in range(BLOCKS)],
                    axis=1,
                )
                for q in range(QUADS)
            ],
            axis=0,
        )
        for side, w in enumerate((wg, wu)):
            product = dot_t(x, w[...])
            for owner in range(n_rep):
                share = product[quarter * owner : quarter * (owner + 1)]
                part[side, c, owner] = share
                part16[side, c, owner] = share.astype(BF16)
        start(far(c))
        start(near(c))

    def add_on(c):
        arrive(far(c))
        relay[0, c] = (part[0, c, right] + far_in[0, c].astype(F32)).astype(BF16)
        relay[1, c] = (part[1, c, left] + far_in[1, c].astype(F32)).astype(BF16)
        start(relayed(c))

    def activate(c):
        arrive(near(c))
        arrive(relayed(c))
        gate = part[0, c, rep] + near_in[0, c].astype(F32) + relay_in[0, c].astype(F32)
        up = part[1, c, rep] + near_in[1, c].astype(F32) + relay_in[1, c].astype(F32)
        hid[c, rep] = (gate / (1.0 + jnp.exp(-gate)) * up).astype(BF16)
        start(hidden_out(c))

    def forward(c):
        arrive(hidden_in(c))
        start(onward(c))

    def down(c):
        arrive(onward_in(c))
        rows2d = dot(hid[c].reshape(n_rep * quarter, ff), wd[...]).astype(BF16)
        pack(rows2d, back, c)

        for v in range(n_z):

            @pl.when(c == v)
            def _(v=v):
                deliver(v, -1, back, home, back_sem, home_sem)

    @pl.loop(0, n_z + STAGES - 1)
    def _(i):
        for age, stage in ((4, down), (3, forward), (2, activate), (1, add_on), (0, multiply)):

            @pl.when((i >= age) & (i < n_z + age))
            def _(age=age, stage=stage):
                stage(i - age)

    slot, prob = slot_t[...].T, prob_t[...].T
    mix = jnp.concatenate(
        [jnp.where(slot == float(s), prob, 0.0) for s in range(CAP)], axis=1
    )
    high = mix.astype(BF16)
    low = (mix - high.astype(F32)).astype(BF16)
    @pl.loop(0, n_z)
    def _(c):
        group = home.at[pl.ds(c * SPAN, SPAN)]
        pltpu.make_async_copy(group, group, home_sem.at[c]).wait()
        tiles = unpack(home, c)
        for q in range(QUADS):
            for s in range(4):
                for b in range(BLOCKS):
                    table[
                        pl.ds((4 * q + s) * experts + c * SPAN, SPAN), LANES * b : LANES * (b + 1)
                    ] = tiles[64 * b + 16 * s : 64 * b + 16 * s + 16, LANES * q : LANES * (q + 1)]

    out[...] = (dot(high, table[...]) + dot(low, table[...])).astype(BF16)

    sent = send.at[pl.ds(1, experts - 1)]
    pltpu.make_async_copy(sent, sent, send_sem).wait()
    returned = back.at[pl.ds(1, experts - 1)]
    pltpu.make_async_copy(returned, returned, back_sem).wait()

    @pl.loop(0, n_z)
    def _(c):
        for copies in (far(c), near(c), relayed(c), hidden_out(c), onward(c)):
            for copy in copies:
                copy.wait_send()


def local(sizes, tokens, expert_ids, route_weights, w_gate, w_up, w_down):
    n_z, n_y, n_rep = sizes
    experts = n_z * SPAN
    rows, width = tokens.shape
    ff = w_gate.shape[1]
    quarter = SPAN * CAP // n_rep
    messages = pltpu.VMEM((experts, QUADS, SPAN, LANES), BF16)
    pair = pltpu.VMEM((2, n_z, quarter, ff), BF16)
    vmem = pl.BlockSpec(memory_space=pltpu.VMEM)
    anywhere = pl.BlockSpec(memory_space=pl.ANY)
    return pl.pallas_call(
        functools.partial(kernel, sizes),
        out_shape=jax.ShapeDtypeStruct((rows, width), BF16),
        in_specs=[vmem] * 3 + [anywhere] * 3,
        out_specs=vmem,
        scratch_shapes=[
            pltpu.VMEM((ff, width), BF16),
            pltpu.VMEM((ff, width), BF16),
            pltpu.VMEM((ff, width), BF16),
            pltpu.VMEM((256, 256), BF16),
            pltpu.VMEM((256, 256), BF16),
            pltpu.VMEM((experts, rows), F32),
            pltpu.VMEM((experts, rows), F32),
            messages,
            messages,
            messages,
            messages,
            pltpu.VMEM((CAP * experts, width), BF16),
            pltpu.VMEM((2, n_z, n_rep, quarter, ff), F32),
            pltpu.VMEM((2, n_z, n_rep, quarter, ff), BF16),
            pair,
            pair,
            pair,
            pair,
            pltpu.VMEM((n_z, n_rep, quarter, ff), BF16),
            pltpu.SemaphoreType.DMA((3,)),
            pltpu.SemaphoreType.DMA,
            pltpu.SemaphoreType.DMA((n_z,)),
            pltpu.SemaphoreType.DMA,
            pltpu.SemaphoreType.DMA((n_z,)),
            pltpu.SemaphoreType.DMA((10, n_z)),
            pltpu.SemaphoreType.DMA((10, n_z)),
        ],
        compiler_params=pltpu.CompilerParams(
            collective_id=0, has_side_effects=True, vmem_limit_bytes=58 * 1024 * 1024
        ),
    )(tokens, expert_ids.T, route_weights.T, w_gate, w_up, w_down)


def solution(mesh):
    n_rep, experts = mesh.shape["rep"], mesh.shape["exp"]
    sizes = (experts // SPAN, SPAN // CORES, n_rep)
    return jax.shard_map(
        functools.partial(local, sizes),
        mesh=mesh,
        in_specs=(
            P("exp", "rep"),
            P("exp", None),
            P("exp", None),
            P("exp", None, "rep"),
            P("exp", None, "rep"),
            P("exp", None, "rep"),
        ),
        out_specs=P("exp", "rep"),
        check_vma=False,
    )
```

```python
import functools

import jax
import jax.numpy as jnp
from jax import lax
from jax.experimental import pallas as pl
from jax.experimental.pallas import tpu as pltpu
from jax.sharding import PartitionSpec as P

MESH = pl.DeviceIdType.MESH
BF16 = jnp.bfloat16
F32 = jnp.float32
CAP = 12
QUADS = 3
SPAN = 16
LANES = 128
BLOCKS = 4
CORES = 2
STAGES = 5


def chunks_of(n_z, n_y):
    if n_z != n_y:
        return [[((i + v) % n_z, i) for i in range(n_y)] for v in range(n_z)]

    def far(offset):
        return min(offset, n_z - offset)

    left = sorted(
        ((z, y) for z in range(n_z) for y in range(n_y)),
        key=lambda p: (far(p[0]) + far(p[1]), abs(far(p[0]) - far(p[1])), p),
    )
    chunks = [[] for _ in range(n_z)]
    chunks[-1], chunks[0] = left[:n_y], left[n_y : 2 * n_y]
    for z, y in reversed(left[2 * n_y :]):

        def cost(chunk):
            along_z = sum(far(p[0]) for p in chunk) + far(z)
            along_y = sum(far(p[1]) for p in chunk) + far(y)
            same = sum((p[0] == z) + (p[1] == y) for p in chunk)
            return along_z**2 + along_y**2 + 40 * same

        open_chunks = [chunk for chunk in chunks[1:-1] if len(chunk) < n_y]
        min(open_chunks, key=cost).append((z, y))
    return [sorted(chunk, key=lambda p: (p[1], p[0])) for chunk in chunks]


def dot(a, b):
    return jnp.dot(a, b, preferred_element_type=F32)


def dot_t(a, b):
    return lax.dot_general(a, b, (((1,), (1,)), ((), ())), preferred_element_type=F32)


def kernel(
    sizes,
    tok,
    ids,
    route,
    wg_any,
    wu_any,
    wd_any,
    out,
    wg,
    wu,
    wd,
    perm,
    perm_t,
    slot_t,
    prob_t,
    send,
    recv,
    back,
    home,
    table,
    part,
    part16,
    far_in,
    near_in,
    relay,
    relay_in,
    hid,
    w_sem,
    send_sem,
    recv_sem,
    back_sem,
    home_sem,
    x_send,
    x_recv,
):
    n_z, n_y, n_rep = sizes
    experts = n_z * SPAN
    ff = wg.shape[0]
    half = ff // 2
    quarter = SPAN * CAP // n_rep
    me, rep = lax.axis_index("exp"), lax.axis_index("rep")
    my_z, my_y, my_c = lax.div(me, SPAN), lax.rem(lax.div(me, CORES), n_y), lax.rem(me, CORES)
    right, left, opp = (lax.rem(rep + step, n_rep) for step in (1, n_rep - 1, 2))

    way = [1 - 2 * my_c, 2 * my_c - 1]

    out_ways, back_ways = [way[0]] * CORES, [-way[0], -way[1]]
    chunks = chunks_of(n_z, n_y)

    def levels(ways):
        return (
            [[lax.rem(my_z + n_z + w * step, n_z) * SPAN for step in range(n_z)] for w in ways],
            [
                [
                    lax.rem(my_y + n_y + w * step, n_y) * CORES + lax.rem(my_c + flip, CORES)
                    for step in range(n_y)
                ]
                for flip, w in enumerate(ways)
            ],
        )

    parts = {1: levels(out_ways), -1: levels(back_ways)}

    def each(v, sign, act):
        in_z, in_y = parts[sign]
        for h in sorted(range(SPAN), key=lambda h: ((h // 2) * 3 + (h % 2) * 4) % 8 * 2 + h % 2):
            (z, y), flip = chunks[v][h // CORES], h % CORES
            if z or y or flip:
                act(v * SPAN + h, in_z[flip][z] + in_y[flip][y])

    barrier = pltpu.get_barrier_semaphore()

    def greet(k, device):
        pl.semaphore_signal(barrier, inc=1, device_id={"exp": device}, device_id_type=MESH)

    for v in (*range(1, n_z), 0):
        each(v, 1, greet)

    for side in (left, right):
        pl.semaphore_signal(barrier, inc=1, device_id={"rep": side}, device_id_type=MESH)

    weights = [
        pltpu.make_async_copy(src.at[0], dst, w_sem.at[i])
        for i, (src, dst) in enumerate(((wg_any, wg), (wu_any, wu), (wd_any, wd)))
    ]
    for copy in weights:
        copy.start()

    row = lax.broadcasted_iota(jnp.int32, (256, 256), 0)
    col = lax.broadcasted_iota(jnp.int32, (256, 256), 1)
    perm[...] = (
        col == (row & 3) * 64 + ((row >> 2) & 3) * 16 + (row >> 4)
    ).astype(F32).astype(BF16)
    perm_t[...] = (
        row == (col & 3) * 64 + ((col >> 2) & 3) * 16 + (col >> 4)
    ).astype(F32).astype(BF16)

    chosen = ids[...]
    rows = chosen.shape[1]
    off_z = (way[0] * ((chosen >> 4) - my_z)) & (n_z - 1)
    off_y = (way[0] * (((chosen >> 1) & (n_y - 1)) - my_y)) & (n_y - 1)
    off_c = ((chosen & 1) - my_c + CORES) & 1
    number = off_c
    for v, chunk in enumerate(chunks):
        for i, (z, y) in enumerate(chunk):
            number = number + jnp.where(
                off_z * n_y + off_y == z * n_y + y, v * SPAN + i * CORES, 0
            )
    probs = route[...] / jnp.sum(route[...], axis=0, keepdims=True)
    place = lax.broadcasted_iota(jnp.int32, (experts, rows), 0)
    named = jnp.zeros((experts, rows), F32)
    prob = jnp.zeros((experts, rows), F32)
    for j in range(chosen.shape[0]):
        hit = number[j : j + 1, :] == place
        named = named + jnp.where(hit, 1.0, 0.0)
        prob = prob + jnp.where(hit, probs[j : j + 1, :], 0.0)
    t_row = lax.broadcasted_iota(jnp.int32, (rows, rows), 0)
    t_col = lax.broadcasted_iota(jnp.int32, (rows, rows), 1)
    earlier = (t_row < t_col).astype(F32).astype(BF16)
    slot_t[...] = jnp.where(named > 0.5, dot(named.astype(BF16), earlier), -1.0)
    prob_t[...] = prob

    pl.semaphore_wait(barrier, experts + 1)

    def deliver(v, sign, src, dst, out_sem, in_sem):
        if (0, 0) in chunks[v]:
            own = v * SPAN + CORES * chunks[v].index((0, 0))
            pltpu.make_async_copy(src.at[own], dst.at[own], in_sem.at[v]).start()

        def go(k, device):
            pltpu.make_async_remote_copy(
                src_ref=src.at[k],
                dst_ref=dst.at[k],
                send_sem=out_sem,
                recv_sem=in_sem.at[v],
                device_id={"exp": device},
                device_id_type=MESH,
            ).start()

        each(v, sign, go)

    def pack(rows2d, place, g):
        stacked = jnp.concatenate(
            [
                jnp.concatenate(
                    [rows2d[64 * q : 64 * q + 64, LANES * b : LANES * (b + 1)] for b in range(BLOCKS)],
                    axis=0,
                )
                for q in range(QUADS)
            ],
            axis=1,
        )
        tiles = dot(perm[...], stacked).astype(BF16)
        for q in range(QUADS):
            place[pl.ds(g * SPAN, SPAN), q] = tiles[:, LANES * q : LANES * (q + 1)].reshape(
                SPAN, SPAN, LANES
            )

    def unpack(place, g):
        tiles = jnp.concatenate(
            [place[pl.ds(g * SPAN, SPAN), q].reshape(256, LANES) for q in range(QUADS)], axis=1
        )
        return dot(perm_t[...], tiles).astype(BF16)

    for g in range(n_z):
        slots = slot_t[pl.ds(g * SPAN, SPAN), :]
        onehot = jnp.concatenate(
            [(slots == float(s)).astype(F32).astype(BF16) for s in range(CAP)], axis=0
        )
        pack(dot(onehot, tok[...]).astype(BF16), send, g)

        deliver(g, 1, send, recv, send_sem, recv_sem)

    for copy in weights:
        copy.wait()

    def across(kind, c, src, dst, side):
        return pltpu.make_async_remote_copy(
            src_ref=src,
            dst_ref=dst,
            send_sem=x_send.at[kind, c],
            recv_sem=x_recv.at[kind, c],
            device_id={"rep": side},
            device_id_type=MESH,
        )

    def far(c):
        return (
            across(0, c, part16.at[0, c, opp], far_in.at[0, c], right),
            across(1, c, part16.at[1, c, opp], far_in.at[1, c], left),
        )

    def near(c):
        return (
            across(2, c, part16.at[1, c, right], near_in.at[1, c], right),
            across(3, c, part16.at[0, c, left], near_in.at[0, c], left),
        )

    def relayed(c):
        return (
            across(4, c, relay.at[0, c], relay_in.at[0, c], right),
            across(5, c, relay.at[1, c], relay_in.at[1, c], left),
        )

    def hidden_out(c):
        return (
            across(6, c, hid.at[c, rep], hid.at[c, rep], right),
            across(7, c, hid.at[c, rep], hid.at[c, rep], left),
        )

    def hidden_in(c):
        return (
            across(6, c, hid.at[c, left], hid.at[c, left], right),
            across(7, c, hid.at[c, right], hid.at[c, right], left),
        )

    def onward(c):
        return (
            across(8, c, hid.at[c, left, :, pl.ds(0, half)], hid.at[c, left, :, pl.ds(0, half)], right),
            across(9, c, hid.at[c, right, :, pl.ds(half, half)], hid.at[c, right, :, pl.ds(half, half)], left),
        )

    def onward_in(c):
        return (
            across(8, c, hid.at[c, opp, :, pl.ds(0, half)], hid.at[c, opp, :, pl.ds(0, half)], right),
            across(9, c, hid.at[c, opp, :, pl.ds(half, half)], hid.at[c, opp, :, pl.ds(half, half)], left),
        )

    def start(copies):
        for copy in copies:
            copy.start()

    def arrive(copies):
        for copy in copies:
            copy.wait_recv()

    def multiply(c):
        group = recv.at[pl.ds(c * SPAN, SPAN)]
        pltpu.make_async_copy(group, group, recv_sem.at[c]).wait()
        tiles = unpack(recv, c)
        x = jnp.concatenate(
            [
                jnp.concatenate(
                    [tiles[64 * b : 64 * b + 64, LANES * q : LANES * (q + 1)] for b in range(BLOCKS)],
                    axis=1,
                )
                for q in range(QUADS)
            ],
            axis=0,
        )
        for side, w in enumerate((wg, wu)):
            product = dot_t(x, w[...])
            for owner in range(n_rep):
                share = product[quarter * owner : quarter * (owner + 1)]
                part[side, c, owner] = share
                part16[side, c, owner] = share.astype(BF16)
        start(far(c))
        start(near(c))

    def add_on(c):
        arrive(far(c))
        relay[0, c] = (part[0, c, right] + far_in[0, c].astype(F32)).astype(BF16)
        relay[1, c] = (part[1, c, left] + far_in[1, c].astype(F32)).astype(BF16)
        start(relayed(c))

    def activate(c):
        arrive(near(c))
        arrive(relayed(c))
        gate = part[0, c, rep] + near_in[0, c].astype(F32) + relay_in[0, c].astype(F32)
        up = part[1, c, rep] + near_in[1, c].astype(F32) + relay_in[1, c].astype(F32)
        hid[c, rep] = (gate / (1.0 + jnp.exp(-gate)) * up).astype(BF16)
        start(hidden_out(c))

    def forward(c):
        arrive(hidden_in(c))
        start(onward(c))

    def down(c):
        arrive(onward_in(c))
        rows2d = dot(hid[c].reshape(n_rep * quarter, ff), wd[...]).astype(BF16)
        pack(rows2d, back, c)

        for v in range(n_z):

            @pl.when(c == v)
            def _(v=v):
                deliver(v, -1, back, home, back_sem, home_sem)

    @pl.loop(0, n_z + STAGES - 1)
    def _(i):
        for age, stage in ((4, down), (3, forward), (2, activate), (1, add_on), (0, multiply)):

            @pl.when((i >= age) & (i < n_z + age))
            def _(age=age, stage=stage):
                stage(i - age)

    slot, prob = slot_t[...].T, prob_t[...].T
    mix = jnp.concatenate(
        [jnp.where(slot == float(s), prob, 0.0) for s in range(CAP)], axis=1
    )
    high = mix.astype(BF16)
    low = (mix - high.astype(F32)).astype(BF16)
    @pl.loop(0, n_z)
    def _(c):
        group = home.at[pl.ds(c * SPAN, SPAN)]
        pltpu.make_async_copy(group, group, home_sem.at[c]).wait()
        tiles = unpack(home, c)
        for q in range(QUADS):
            for s in range(4):
                for b in range(BLOCKS):
                    table[
                        pl.ds((4 * q + s) * experts + c * SPAN, SPAN), LANES * b : LANES * (b + 1)
                    ] = tiles[64 * b + 16 * s : 64 * b + 16 * s + 16, LANES * q : LANES * (q + 1)]

    both = dot(jnp.concatenate([high, low], axis=0), table[...])
    out[...] = (both[: both.shape[0] // 2] + both[both.shape[0] // 2 :]).astype(BF16)

    sent = send.at[pl.ds(1, experts - 1)]
    pltpu.make_async_copy(sent, sent, send_sem).wait()
    returned = back.at[pl.ds(1, experts - 1)]
    pltpu.make_async_copy(returned, returned, back_sem).wait()

    @pl.loop(0, n_z)
    def _(c):
        for copies in (far(c), near(c), relayed(c), hidden_out(c), onward(c)):
            for copy in copies:
                copy.wait_send()


def local(sizes, tokens, expert_ids, route_weights, w_gate, w_up, w_down):
    n_z, n_y, n_rep = sizes
    experts = n_z * SPAN
    rows, width = tokens.shape
    ff = w_gate.shape[1]
    quarter = SPAN * CAP // n_rep
    messages = pltpu.VMEM((experts, QUADS, SPAN, LANES), BF16)
    pair = pltpu.VMEM((2, n_z, quarter, ff), BF16)
    vmem = pl.BlockSpec(memory_space=pltpu.VMEM)
    anywhere = pl.BlockSpec(memory_space=pl.ANY)
    return pl.pallas_call(
        functools.partial(kernel, sizes),
        out_shape=jax.ShapeDtypeStruct((rows, width), BF16),
        in_specs=[vmem] * 3 + [anywhere] * 3,
        out_specs=vmem,
        scratch_shapes=[
            pltpu.VMEM((ff, width), BF16),
            pltpu.VMEM((ff, width), BF16),
            pltpu.VMEM((ff, width), BF16),
            pltpu.VMEM((256, 256), BF16),
            pltpu.VMEM((256, 256), BF16),
            pltpu.VMEM((experts, rows), F32),
            pltpu.VMEM((experts, rows), F32),
            messages,
            messages,
            messages,
            messages,
            pltpu.VMEM((CAP * experts, width), BF16),
            pltpu.VMEM((2, n_z, n_rep, quarter, ff), F32),
            pltpu.VMEM((2, n_z, n_rep, quarter, ff), BF16),
            pair,
            pair,
            pair,
            pair,
            pltpu.VMEM((n_z, n_rep, quarter, ff), BF16),
            pltpu.SemaphoreType.DMA((3,)),
            pltpu.SemaphoreType.DMA,
            pltpu.SemaphoreType.DMA((n_z,)),
            pltpu.SemaphoreType.DMA,
            pltpu.SemaphoreType.DMA((n_z,)),
            pltpu.SemaphoreType.DMA((10, n_z)),
            pltpu.SemaphoreType.DMA((10, n_z)),
        ],
        compiler_params=pltpu.CompilerParams(
            collective_id=0, has_side_effects=True, vmem_limit_bytes=58 * 1024 * 1024
        ),
    )(tokens, expert_ids.T, route_weights.T, w_gate, w_up, w_down)


def solution(mesh):
    n_rep, experts = mesh.shape["rep"], mesh.shape["exp"]
    sizes = (experts // SPAN, SPAN // CORES, n_rep)
    return jax.shard_map(
        functools.partial(local, sizes),
        mesh=mesh,
        in_specs=(
            P("exp", "rep"),
            P("exp", None),
            P("exp", None),
            P("exp", None, "rep"),
            P("exp", None, "rep"),
            P("exp", None, "rep"),
        ),
        out_specs=P("exp", "rep"),
        check_vma=False,
    )
```
